512 devices in a mesh: grp: 16 (over z, core), dom: 32 (over x, y).
Axes of the slice: x: 4, y: 8, z: 8, core: 2. Of those that a mesh axis runs over, the one named last changes fastest.
Arguments:
- leaf_load: bfloat16 [32, 16, 1024, 128], P('dom', 'grp'), may hold values from -6 to 6
- leaf_map: bfloat16 [32, 16, 1024, 1024], P('dom', 'grp'), may hold values from -0.1875 to 0.1875
- group_map: bfloat16 [32, 4096, 4096], P('dom', 'grp'), may hold values from -0.09375 to 0.09375
- node_index: int32 [32, 16, 1024], P('dom', 'grp'), may hold values from 0 to 4095, as said below
- west_coupling: float32 [32, 256, 256], P('dom'), may hold values from -1.5 to 1.5
- east_coupling: float32 [32, 256, 256], P('dom'), may hold values from -1.5 to 1.5
Outputs:
- leaf_solution: bfloat16 [32, 16, 1024, 128], P('dom', 'grp')
The draws below stay inside these ranges and needn't reach their ends.
Inputs may be any that keep to these rules, and one draw needn't show every extreme that they name: `node_index`: each leaf's list names 1024 different interface nodes of its group.
All inputs are finite; a program needn't handle non-finite values.
Results may differ from the reference program's by a relative error of at most 0.015.
Values may be sent and summed in bfloat16 or wider, within the bound.
No kernel may reach another device: no remote copies, remote signals or barrier semaphores. Data moves between devices by JAX's collectives and lax.ppermute only.
A program may use at most 128 MiB of HBM per device.

```python
import jax
import jax.numpy as jnp
from jax import lax

B = 1024
IF = 4096
NB = 256
R = 128
LEAVES = 16
DOMS = 32


def draw_node_index(key, part):
    subkeys = jax.random.split(key, DOMS * LEAVES)
    chosen = jax.vmap(lambda single: jax.random.permutation(single, IF)[:B])(subkeys)
    return chosen.reshape(DOMS, LEAVES, B).astype(jnp.int32)


def block_levels(stream_key, extent, cuts, least, largest):
    def one(position, parts):
        steps = jax.random.uniform(jax.random.fold_in(jax.random.fold_in(stream_key, 6), position), (parts,), jnp.float32, least / len(cuts), largest / len(cuts))
        return jnp.repeat(jnp.exp(steps), extent[position] // parts).reshape((-1,) + (1,) * (len(extent) - position - 1))

    gain = one(*cuts[0])
    for cut in cuts[1:]:
        gain = gain * one(*cut)
    return gain


def normal_values(stream_key, shape, width, bound, shards=(), dtype=jnp.bfloat16):
    entries = width * jax.random.normal(stream_key, shape, jnp.float32)
    if shards:
        entries = entries * block_levels(stream_key, shape, shards, -0.22, 0.18)
    return jnp.clip(entries, -bound, bound).astype(dtype)


def setup_inputs(seed: int = 0) -> dict:
    key_of = jax.random.split(jax.random.key(seed), 7)
    leaf_load = normal_values(key_of[0], (DOMS, LEAVES, B, R), 1.0, 6.0, ((0, 32), (1, 16)))
    leaf_map = normal_values(key_of[1], (DOMS, LEAVES, B, B), B ** -0.5, 0.1875, ((0, 32), (1, 16)))
    group_map = normal_values(key_of[2], (DOMS, IF, IF), IF ** -0.5, 0.09375, ((0, 32), (1, 16)))
    node_index = draw_node_index(jax.random.fold_in(key_of[6], 71), 0)
    west_coupling = normal_values(key_of[4], (DOMS, NB, NB), (NB * NB * 10 // (9 * IF)) ** -0.5, 1.5, ((0, 32),), jnp.float32)
    east_coupling = normal_values(key_of[5], (DOMS, NB, NB), (NB * NB * 10 // (9 * IF)) ** -0.5, 1.5, ((0, 32),), jnp.float32)
    return dict(leaf_load=leaf_load, leaf_map=leaf_map, group_map=group_map, node_index=node_index, west_coupling=west_coupling, east_coupling=east_coupling)


def reference(leaf_load, leaf_map, group_map, node_index, west_coupling, east_coupling):
    exact_mode = lax.Precision.HIGHEST
    stride = IF // NB
    initial_rows = []
    for domain in range(DOMS):
        contrib = jnp.einsum("lij,ljr->lir", leaf_map[domain].astype(jnp.float32), leaf_load[domain].astype(jnp.float32)).astype(jnp.bfloat16)
        summed = jnp.zeros((IF, R), jnp.float32).at[node_index[domain].reshape(-1)].add(contrib.reshape(-1, R).astype(jnp.float32))
        initial_rows.append(jnp.dot(group_map[domain], summed.astype(jnp.bfloat16), preferred_element_type=jnp.float32))
    carried = jnp.zeros((NB, R), jnp.float32)
    swept_rows = []
    for domain in range(DOMS):
        coupled = jnp.dot(west_coupling[domain], carried, precision=exact_mode)
        columns = group_map[domain][:, 0::stride].astype(jnp.float32)
        current = initial_rows[domain] + jnp.dot(columns, coupled, precision=exact_mode)
        swept_rows.append(current)
        carried = current[1::stride]
    carried = jnp.zeros((NB, R), jnp.float32)
    final_rows = [None] * DOMS
    for domain in range(DOMS - 1, -1, -1):
        coupled = jnp.dot(east_coupling[domain], carried, precision=exact_mode)
        columns = group_map[domain][:, 1::stride].astype(jnp.float32)
        current = swept_rows[domain] + jnp.dot(columns, coupled, precision=exact_mode)
        final_rows[domain] = current
        carried = current[0::stride]
    outputs = []
    for domain in range(DOMS):
        solution_rows = final_rows[domain].astype(jnp.bfloat16)
        picked = solution_rows[node_index[domain]]
        result = jnp.einsum("lbi,lbr->lir", leaf_map[domain].astype(jnp.float32), picked.astype(jnp.float32)) + leaf_load[domain].astype(jnp.float32)
        outputs.append(result.astype(jnp.bfloat16))
    return jnp.stack(outputs)
```

```python
import functools

import jax
import jax.numpy as jnp
from jax import lax
from jax.experimental import pallas as pl
from jax.experimental.pallas import tpu as pltpu
from jax.sharding import Mesh
from jax.sharding import PartitionSpec as P

F32 = jnp.float32
BF16 = jnp.bfloat16
GRP = ("z", "c")
NT = (((1,), (1,)), ((), ()))
VM = pl.BlockSpec(memory_space=pltpu.VMEM)
SM = pl.BlockSpec(memory_space=pltpu.SMEM)
PARAMS = pltpu.CompilerParams(vmem_limit_bytes=56 * 1024 * 1024)


def call(kernel, name, outs, scratch, smem, cost, *args):
    specs = [SM] * smem + [VM] * (len(args) - smem)
    flops, moved = cost
    return pl.pallas_call(
        kernel,
        name=name,
        out_shape=outs,
        in_specs=specs,
        out_specs=jax.tree.map(lambda _: VM, outs),
        scratch_shapes=scratch,
        compiler_params=PARAMS,
        cost_estimate=pl.CostEstimate(flops=flops, bytes_accessed=moved, transcendentals=0),
    )(*args)


def spread_rows(pos, map_ref, load_ref, keep_ref, send_ref, contrib, rows):
    contrib[...] = (
        jnp.dot(map_ref[...], load_ref[...], preferred_element_type=F32).astype(BF16).astype(F32)
    )
    rows[...] = jnp.zeros_like(rows)
    count = contrib.shape[0]
    unroll = 16

    def some(turn, carry):
        base = pl.multiple_of(turn * unroll, unroll)
        for k in range(unroll):
            rows[pl.ds(pos[base + k], 1), :] = contrib[pl.ds(base + k, 1), :]
        return carry

    lax.fori_loop(0, count // unroll, some, 0)
    half = keep_ref.shape[0]
    keep_ref[...] = rows[:half].astype(BF16)
    send_ref[...] = rows[half:].astype(BF16)


def first_rows(core, map_ref, own_ref, other_ref, initial_ref, faces_ref, acc, *, width, stride):
    side = core[0]
    pairs = own_ref.shape[0] // width
    acc[...] = jnp.zeros_like(acc)
    for z in range(pairs):
        mine = pl.ds(pl.multiple_of((2 * z + side) * width, width), width)
        theirs = pl.ds(pl.multiple_of((2 * z + 1 - side) * width, width), width)
        block = slice(z * width, (z + 1) * width)
        acc[...] += jnp.dot(map_ref[:, mine], own_ref[block], preferred_element_type=F32)
        acc[...] += jnp.dot(map_ref[:, theirs], other_ref[block], preferred_element_type=F32)
    initial_ref[...] = acc[...]
    nodes = acc.shape[0] // stride
    west = acc[pl.ds(0, nodes, stride=stride), :]
    east = acc[pl.ds(1, nodes, stride=stride), :]
    both = jnp.concatenate([east, west], axis=0)
    lanes = both.shape[1]
    peers = faces_ref.shape[0]
    part = lanes // peers
    for g in range(peers):
        turned = both if g == 0 else pltpu.roll(both, lanes - part * g, axis=1)
        faces_ref[g] = turned.astype(BF16)


def face_columns(got_ref, out_ref, order, *, nodes, part):
    peers = got_ref.shape[0]
    for g in range(peers):
        both = got_ref[g].astype(F32)
        order[pl.ds(g * nodes, nodes), :] = both[:nodes]
        order[pl.ds((peers + g) * nodes, nodes), :] = both[nodes:]
    line = order[...].T[:part].astype(BF16)
    for y in range(out_ref.shape[0]):
        out_ref[y] = line


def halves(value):
    high = value.astype(BF16)
    low = (value - high.astype(F32)).astype(BF16)
    return high, low


def exact_right(left, value):
    high, low = halves(value)
    return jnp.dot(left, high, preferred_element_type=F32) + jnp.dot(
        left, low, preferred_element_type=F32
    )


def exact_rows(value, right):
    rows = value.shape[0]
    high, low = halves(value)
    both = lax.dot_general(
        jnp.concatenate([high, low], axis=0), right, NT, preferred_element_type=F32
    )
    return both[:rows] + both[rows:]


def block_maps(place, maps_ref, joined_ref, own_ref, state, right, through):
    count = maps_ref.shape[0]
    n = maps_ref.shape[2]
    here = place[0]
    unit = (
        lax.broadcasted_iota(jnp.int32, (n, n), 0) == lax.broadcasted_iota(jnp.int32, (n, n), 1)
    ).astype(F32)
    state[...] = unit

    def onward(j, carry):
        value = state[...]

        @pl.when(j == here)
        def _():
            own_ref[0:n] = value.astype(own_ref.dtype)

        both = exact_right(maps_ref[j, 0 : 2 * n, :], value)
        state[...] = both[:n]
        through[j] = both[n:]
        return carry

    lax.fori_loop(0, count, onward, 0)
    joined_ref[0:n] = state[...].astype(BF16)
    right[:, 0:n] = unit
    right[:, n : 2 * n] = jnp.zeros((n, n), F32)

    def back(turn, carry):
        j = count - 1 - turn
        value = right[...]

        @pl.when(j == here)
        def _():
            own_ref[n : 2 * n] = value[:, 0:n].astype(own_ref.dtype)
            own_ref[2 * n : 3 * n] = value[:, n : 2 * n].astype(own_ref.dtype)

        both = exact_right(maps_ref[j, 2 * n : 3 * n, :], value)
        right[:, 0:n] = both[:, 0:n]
        right[:, n : 2 * n] = both[:, n : 2 * n] + through[j]
        return carry

    lax.fori_loop(0, count, back, 0)
    joined_ref[n : 2 * n] = right[:, 0:n].astype(BF16)
    joined_ref[2 * n : 3 * n] = right[:, n : 2 * n].astype(BF16)


def block_values(place, faces_ref, maps_ref, ends_ref, own_ref):
    count, part, _ = faces_ref.shape
    n = maps_ref.shape[2]
    here = place[0]
    value = jnp.zeros((part, n), F32)
    sources = []
    for j in range(count):

        @pl.when(here == j)
        def _(value=value):
            own_ref[:, 0:n] = value

        both = exact_rows(value, maps_ref[j, 0 : 2 * n, :]) if j else None
        given = faces_ref[j].astype(F32)
        if j:
            value = given[:, 0:n] + both[:, 0:n]
            sources.append(given[:, n : 2 * n] + both[:, n : 2 * n])
        else:
            value = given[:, 0:n]
            sources.append(given[:, n : 2 * n])
    east = value
    value = jnp.zeros((part, n), F32)
    for j in range(count - 1, -1, -1):

        @pl.when(here == j)
        def _(value=value):
            own_ref[:, n : 2 * n] = value

        value = sources[j] + (
            exact_rows(value, maps_ref[j, 2 * n : 3 * n, :]) if j < count - 1 else 0.0
        )
    ends = jnp.concatenate([east, value], axis=1).astype(BF16)
    for x in range(ends_ref.shape[0]):
        ends_ref[x] = ends


def meet_values(place, ends_ref, joined_ref, maps_ref, own_ref, out_ref, entering):
    count, part, _ = ends_ref.shape
    n = joined_ref.shape[2]
    here = place[0]
    east = jnp.zeros((part, n), F32)
    sources = []
    for b in range(count):

        @pl.when(here == b)
        def _(east=east):
            entering[:, 0:n] = east

        end = ends_ref[b].astype(F32)
        source = end[:, n : 2 * n]
        if b:
            source = source + exact_rows(east, joined_ref[b, 2 * n : 3 * n, :])
        sources.append(source)
        east = end[:, 0:n] + (exact_rows(east, joined_ref[b, 0:n, :]) if b else 0.0)
    west = jnp.zeros((part, n), F32)
    for b in range(count - 1, -1, -1):

        @pl.when(here == b)
        def _(west=west):
            entering[:, n : 2 * n] = west

        west = sources[b] + (
            exact_rows(west, joined_ref[b, n : 2 * n, :]) if b < count - 1 else 0.0
        )
    east = entering[:, 0:n]
    west = entering[:, n : 2 * n]
    own = own_ref[...]
    met_east = own[:, 0:n] + exact_rows(east, maps_ref[0:n])
    met_west = (
        own[:, n : 2 * n]
        + exact_rows(west, maps_ref[n : 2 * n])
        + exact_rows(east, maps_ref[2 * n : 3 * n])
    )
    met = jnp.concatenate([met_east, met_west], axis=1).astype(BF16)
    for g in range(out_ref.shape[0]):
        out_ref[g] = met


def leaf_result(pos, own_ref, other_ref, map_ref, load_ref, out_ref, rows, picked):
    half = own_ref.shape[0]
    rows[0:half] = own_ref[...].astype(F32)
    rows[half : 2 * half] = other_ref[...].astype(F32)
    count = picked.shape[0]
    unroll = 16

    def some(turn, carry):
        base = pl.multiple_of(turn * unroll, unroll)
        for k in range(unroll):
            picked[pl.ds(base + k, 1), :] = rows[pl.ds(pos[base + k], 1), :]
        return carry

    lax.fori_loop(0, count // unroll, some, 0)
    turned = picked[...].T.astype(BF16)
    result = jnp.dot(turned, map_ref[...], preferred_element_type=F32)
    out_ref[...] = (result.T + load_ref[...].astype(F32)).astype(BF16)


def on_device(leaf_load, leaf_map, group_map, node_index, west_coupling, east_coupling):
    local_map, local_load, nodes_of = leaf_map[0, 0], leaf_load[0, 0], node_index[0, 0]
    rows_map, west, east = group_map[0], west_coupling[0], east_coupling[0]
    nz, nc = lax.axis_size("z"), lax.axis_size("c")
    nx, ny = lax.axis_size("x"), lax.axis_size("y")
    peers = nz * nc
    leaf_nodes, columns = local_load.shape
    width, interface = rows_map.shape
    n = west.shape[0]
    stride = interface // n
    nodes = n // peers
    part = columns // peers
    half = interface // nc
    side = lax.axis_index("c")
    core = jnp.reshape(side, (1,)).astype(jnp.int32)
    at_y = jnp.reshape(lax.axis_index("y"), (1,)).astype(jnp.int32)
    at_x = jnp.reshape(lax.axis_index("x"), (1,)).astype(jnp.int32)
    swap = [(0, 1), (1, 0)]

    spot = lax.broadcasted_iota(jnp.int32, (interface, 2 * n), 0)
    want = lax.broadcasted_iota(jnp.int32, (interface, 2 * n), 1)
    want = jnp.where(want < n, want * stride, (want - n) * stride + 1)
    face_map = jnp.dot(rows_map, (spot == want).astype(BF16), preferred_element_type=F32)
    west_high, west_low = halves(west)
    east_high, east_low = halves(east)
    face_low = face_map.astype(BF16)
    coupled = jnp.concatenate(
        [
            jnp.dot(face_low[:, :n], west_high, preferred_element_type=F32)
            + jnp.dot(face_low[:, :n], west_low, preferred_element_type=F32),
            jnp.dot(face_low[:, n:], east_high, preferred_element_type=F32)
            + jnp.dot(face_low[:, n:], east_low, preferred_element_type=F32),
        ],
        axis=1,
    ).astype(BF16)
    steps = coupled.reshape(nodes, stride, 2 * n)
    slices = jnp.concatenate([steps[:, 1, :n], steps[:, 0, :n], steps[:, 0, n:]], axis=0)
    slices = jnp.broadcast_to(slices, (peers,) + slices.shape)
    slices = lax.all_to_all(slices, GRP, 0, 0)
    maps = slices.reshape(peers, 3, nodes, n).transpose(1, 0, 2, 3).reshape(3 * n, n)
    run_maps = lax.all_gather(maps, "y")

    owner = nodes_of // width
    pos = ((owner % nc) ^ side) * half + (owner // nc) * width + nodes_of % width
    keep, send = call(
        spread_rows,
        "spread_rows",
        (jax.ShapeDtypeStruct((half, columns), BF16),) * 2,
        [pltpu.VMEM((leaf_nodes, columns), F32), pltpu.VMEM((interface, columns), F32)],
        1,
        (2 * leaf_nodes * leaf_nodes * columns, 6 * leaf_nodes * leaf_nodes),
        pos,
        local_map,
        local_load,
    )
    got = lax.ppermute(send, "c", swap)
    paired = (keep.astype(F32) + got.astype(F32)).astype(BF16)
    parts = lax.all_to_all(paired.reshape(nz, width, columns), "z", 0, 0)
    loads = jnp.sum(parts.astype(F32), axis=0).astype(BF16)
    loads = lax.all_to_all(jnp.broadcast_to(loads, (nz, width, columns)), "z", 0, 0)
    loads_own = loads.reshape(half, columns)
    loads_other = lax.ppermute(loads_own, "c", swap)

    initial, faces = call(
        functools.partial(first_rows, width=width, stride=stride),
        "first_rows",
        (
            jax.ShapeDtypeStruct((width, columns), F32),
            jax.ShapeDtypeStruct((peers, 2 * nodes, columns), BF16),
        ),
        [pltpu.VMEM((width, columns), F32)],
        1,
        (2 * width * interface * columns, 2 * width * interface),
        core,
        rows_map,
        loads_own,
        loads_other,
    )
    faces = lax.all_to_all(faces, GRP, 0, 0)

    run_maps, loads_own = lax.optimization_barrier((run_maps, loads_own))
    joined, own_maps = call(
        block_maps,
        "block_maps",
        (jax.ShapeDtypeStruct((3 * n, n), BF16), jax.ShapeDtypeStruct((3 * n, n), BF16)),
        [
            pltpu.VMEM((n, n), F32),
            pltpu.VMEM((n, 2 * n), F32),
            pltpu.VMEM((ny, n, n), F32),
        ],
        1,
        (16 * ny * n**3, 6 * ny * n * n),
        at_y,
        run_maps,
    )
    all_joined = lax.all_gather(joined, "x")

    line = call(
        functools.partial(face_columns, nodes=nodes, part=part),
        "face_columns",
        jax.ShapeDtypeStruct((ny, part, 2 * n), BF16),
        [pltpu.VMEM((2 * n, columns), F32)],
        0,
        (1000, 4 * n * columns),
        faces,
    )
    line = lax.all_to_all(line, "y", 0, 0)
    ends, own_values = call(
        block_values,
        "block_values",
        (
            jax.ShapeDtypeStruct((nx, part, 2 * n), BF16),
            jax.ShapeDtypeStruct((part, 2 * n), F32),
        ),
        [],
        1,
        (12 * ny * n * n * 16, 6 * ny * n * n),
        at_y,
        line,
        run_maps,
    )
    ends = lax.all_to_all(ends, "x", 0, 0)
    met = call(
        meet_values,
        "meet_values",
        jax.ShapeDtypeStruct((peers, part, 2 * n), BF16),
        [pltpu.VMEM((part, 2 * n), F32)],
        1,
        (12 * nx * n * n * 16, 6 * nx * n * n),
        at_x,
        ends,
        all_joined,
        own_maps,
        own_values,
    )
    met = lax.all_to_all(met, GRP, 0, 0).reshape(columns, 2 * n)

    final = initial + lax.dot_general(coupled, met, NT, preferred_element_type=F32)
    final = jnp.broadcast_to(final.astype(BF16), (nz, width, columns))
    final_own = lax.all_to_all(final, "z", 0, 0).reshape(half, columns)
    final_other = lax.ppermute(final_own, "c", swap)
    result = call(
        leaf_result,
        "leaf_result",
        jax.ShapeDtypeStruct((leaf_nodes, columns), BF16),
        [pltpu.VMEM((interface, columns), F32), pltpu.VMEM((leaf_nodes, columns), F32)],
        1,
        (2 * leaf_nodes * leaf_nodes * columns, 2 * leaf_nodes * leaf_nodes),
        pos,
        final_own,
        final_other,
        local_map,
        local_load,
    )
    return result[None, None]


SPLITS = {(16, 32): (8, 2, 4, 8)}


def solution(mesh):
    shape = SPLITS.get(tuple(mesh.devices.shape), (2, 2, 2, 2))
    split = Mesh(mesh.devices.reshape(shape), ("z", "c", "x", "y"))
    grp, dom = ("z", "c"), ("x", "y")
    return jax.shard_map(
        on_device,
        mesh=split,
        in_specs=(
            P(dom, grp, None, None),
            P(dom, grp, None, None),
            P(dom, grp, None),
            P(dom, grp, None),
            P(dom, None, None),
            P(dom, None, None),
        ),
        out_specs=P(dom, grp, None, None),
        check_vma=False,
    )
```

```python
import functools

import jax
import jax.numpy as jnp
from jax import lax
from jax.experimental import pallas as pl
from jax.experimental.pallas import tpu as pltpu
from jax.sharding import Mesh
from jax.sharding import PartitionSpec as P


F32 = jnp.float32
BF16 = jnp.bfloat16
GRP = ("z", "c")
NT = (((1,), (1,)), ((), ()))
VM = pl.BlockSpec(memory_space=pltpu.VMEM)
SM = pl.BlockSpec(memory_space=pltpu.SMEM)
PARAMS = pltpu.CompilerParams(vmem_limit_bytes=16 * 1024 * 1024)


def call(kernel, outs, scratch, smem, cost, *args):
    specs = [SM] * smem + [VM] * (len(args) - smem)
    flops, moved = cost
    return pl.pallas_call(
        kernel,
        out_shape=outs,
        in_specs=specs,
        out_specs=jax.tree.map(lambda _: VM, outs),
        scratch_shapes=scratch,
        compiler_params=PARAMS,
        cost_estimate=pl.CostEstimate(flops=flops, bytes_accessed=moved, transcendentals=0),
    )(*args)


def moved(value, axis):
    return lax.all_to_all(value, axis, 0, 0)


def spread_rows(pos, map_ref, load_ref, keep_ref, send_ref, contrib, rows):
    contrib[...] = (
        jnp.dot(map_ref[...], load_ref[...], preferred_element_type=F32).astype(BF16).astype(F32)
    )
    rows[...] = jnp.zeros_like(rows)
    count = contrib.shape[0]
    unroll = 16

    def some(turn, carry):
        base = pl.multiple_of(turn * unroll, unroll)
        for k in range(unroll):
            rows[pl.ds(pos[base + k], 1), :] = contrib[pl.ds(base + k, 1), :]
        return carry

    lax.fori_loop(0, count // unroll, some, 0)
    half = keep_ref.shape[0]
    keep_ref[...] = rows[:half].astype(BF16)
    send_ref[...] = rows[half:].astype(BF16)


def face_parts(parts_ref, rows_ref, loads_ref, out_ref, order):
    total = parts_ref[0].astype(F32)
    for z in range(1, parts_ref.shape[0]):
        total = total + parts_ref[z].astype(F32)
    loads = total.astype(BF16)
    for z in range(loads_ref.shape[0]):
        loads_ref[z] = loads
    peers, both, _ = rows_ref.shape
    nodes = both // 2
    for g in range(peers):
        order[g * nodes : (g + 1) * nodes] = rows_ref[g, 0:nodes]
        order[(peers + g) * nodes : (peers + g + 1) * nodes] = rows_ref[g, nodes:both]
    lines = lax.dot_general(total.T.astype(BF16), order[...], NT, preferred_element_type=F32)
    part = out_ref.shape[1]
    for g in range(peers):
        out_ref[g] = lines[g * part : (g + 1) * part].astype(BF16)


def face_sum(got_ref, out_ref):
    total = got_ref[0].astype(F32)
    for g in range(1, got_ref.shape[0]):
        total = total + got_ref[g].astype(F32)
    line = total.astype(BF16)
    for y in range(out_ref.shape[0]):
        out_ref[y] = line


def first_rows(core, map_ref, own_ref, other_ref, initial_ref, *, width):
    side = core[0]
    pairs = own_ref.shape[0] // width
    total = None
    for z in range(pairs):
        mine = pl.ds(pl.multiple_of((2 * z + side) * width, width), width)
        theirs = pl.ds(pl.multiple_of((2 * z + 1 - side) * width, width), width)
        block = slice(z * width, (z + 1) * width)
        both = jnp.dot(map_ref[:, mine], own_ref[block], preferred_element_type=F32) + jnp.dot(
            map_ref[:, theirs], other_ref[block], preferred_element_type=F32
        )
        total = both if total is None else total + both
    initial_ref[...] = total


def halves(value):
    high = value.astype(BF16)
    low = (value - high.astype(F32)).astype(BF16)
    return high, low


def exact_right(left, value):
    high, low = halves(value)
    return jnp.dot(left, high, preferred_element_type=F32) + jnp.dot(
        left, low, preferred_element_type=F32
    )


def exact_rows(value, right):
    rows = value.shape[0]
    high, low = halves(value)
    both = lax.dot_general(
        jnp.concatenate([high, low], axis=0), right, NT, preferred_element_type=F32
    )
    return both[:rows] + both[rows:]


def block_maps(place, maps_ref, joined_ref, own_ref, state, right, through):
    count = maps_ref.shape[0]
    n = maps_ref.shape[2]
    here = place[0]
    unit = (
        lax.broadcasted_iota(jnp.int32, (n, n), 0) == lax.broadcasted_iota(jnp.int32, (n, n), 1)
    ).astype(F32)
    state[...] = unit

    def onward(j, carry):
        value = state[...]

        @pl.when(j == here)
        def _():
            own_ref[0:n] = value.astype(own_ref.dtype)

        both = exact_right(maps_ref[j, 0 : 2 * n, :], value)
        state[...] = both[:n]
        through[j] = both[n:]
        return carry

    lax.fori_loop(0, count, onward, 0)
    joined_ref[0:n] = state[...].astype(BF16)
    right[:, 0:n] = unit
    right[:, n : 2 * n] = jnp.zeros((n, n), F32)

    def back(turn, carry):
        j = count - 1 - turn
        value = right[...]

        @pl.when(j == here)
        def _():
            own_ref[n : 2 * n] = value[:, 0:n].astype(own_ref.dtype)
            own_ref[2 * n : 3 * n] = value[:, n : 2 * n].astype(own_ref.dtype)

        both = exact_right(maps_ref[j, 2 * n : 3 * n, :], value)
        right[:, 0:n] = both[:, 0:n]
        right[:, n : 2 * n] = both[:, n : 2 * n] + through[j]
        return carry

    lax.fori_loop(0, count, back, 0)
    joined_ref[n : 2 * n] = right[:, 0:n].astype(BF16)
    joined_ref[2 * n : 3 * n] = right[:, n : 2 * n].astype(BF16)


def block_values(place, faces_ref, maps_ref, ends_ref, own_ref):
    count, part, _ = faces_ref.shape
    n = maps_ref.shape[2]
    here = place[0]
    value = jnp.zeros((part, n), F32)
    sources = []
    for j in range(count):

        @pl.when(here == j)
        def _(value=value):
            own_ref[:, 0:n] = value

        both = exact_rows(value, maps_ref[j, 0 : 2 * n, :]) if j else None
        given = faces_ref[j].astype(F32)
        if j:
            value = given[:, 0:n] + both[:, 0:n]
            sources.append(given[:, n : 2 * n] + both[:, n : 2 * n])
        else:
            value = given[:, 0:n]
            sources.append(given[:, n : 2 * n])
    east = value
    value = jnp.zeros((part, n), F32)
    for j in range(count - 1, -1, -1):

        @pl.when(here == j)
        def _(value=value):
            own_ref[:, n : 2 * n] = value

        value = sources[j] + (
            exact_rows(value, maps_ref[j, 2 * n : 3 * n, :]) if j < count - 1 else 0.0
        )
    ends = jnp.concatenate([east, value], axis=1).astype(BF16)
    for x in range(ends_ref.shape[0]):
        ends_ref[x] = ends


def meet_values(place, ends_ref, joined_ref, maps_ref, own_ref, out_ref, entering):
    count, part, _ = ends_ref.shape
    n = joined_ref.shape[2]
    here = place[0]
    east = jnp.zeros((part, n), F32)
    sources = []
    for b in range(count):

        @pl.when(here == b)
        def _(east=east):
            entering[:, 0:n] = east

        end = ends_ref[b].astype(F32)
        source = end[:, n : 2 * n]
        if b:
            source = source + exact_rows(east, joined_ref[b, 2 * n : 3 * n, :])
        sources.append(source)
        east = end[:, 0:n] + (exact_rows(east, joined_ref[b, 0:n, :]) if b else 0.0)
    west = jnp.zeros((part, n), F32)
    for b in range(count - 1, -1, -1):

        @pl.when(here == b)
        def _(west=west):
            entering[:, n : 2 * n] = west

        west = sources[b] + (
            exact_rows(west, joined_ref[b, n : 2 * n, :]) if b < count - 1 else 0.0
        )
    east = entering[:, 0:n]
    west = entering[:, n : 2 * n]
    own = own_ref[...]
    met_east = own[:, 0:n] + exact_rows(east, maps_ref[0:n])
    met_west = (
        own[:, n : 2 * n]
        + exact_rows(west, maps_ref[n : 2 * n])
        + exact_rows(east, maps_ref[2 * n : 3 * n])
    )
    met = jnp.concatenate([met_east, met_west], axis=1).astype(BF16)
    for g in range(out_ref.shape[0]):
        out_ref[g] = met


def leaf_result(pos, own_ref, other_ref, map_ref, load_ref, out_ref, rows, picked):
    half = own_ref.shape[0]
    rows[0:half] = own_ref[...].astype(F32)
    rows[half : 2 * half] = other_ref[...].astype(F32)
    count = picked.shape[0]
    unroll = 16

    def some(turn, carry):
        base = pl.multiple_of(turn * unroll, unroll)
        for k in range(unroll):
            picked[pl.ds(base + k, 1), :] = rows[pl.ds(pos[base + k], 1), :]
        return carry

    lax.fori_loop(0, count // unroll, some, 0)
    turned = picked[...].T.astype(BF16)
    result = jnp.dot(turned, map_ref[...], preferred_element_type=F32)
    out_ref[...] = (result.T + load_ref[...].astype(F32)).astype(BF16)


def on_device(leaf_load, leaf_map, group_map, node_index, west_coupling, east_coupling):
    local_map, local_load, nodes_of = leaf_map[0, 0], leaf_load[0, 0], node_index[0, 0]
    rows_map, west, east = group_map[0], west_coupling[0], east_coupling[0]
    nz, nc = lax.axis_size("z"), lax.axis_size("c")
    nx, ny = lax.axis_size("x"), lax.axis_size("y")
    peers = nz * nc
    leaf_nodes, columns = local_load.shape
    width, interface = rows_map.shape
    n = west.shape[0]
    stride = interface // n
    nodes = n // peers
    part = columns // peers
    half = interface // nc
    side = lax.axis_index("c")
    core = jnp.reshape(side, (1,)).astype(jnp.int32)
    at_y = jnp.reshape(lax.axis_index("y"), (1,)).astype(jnp.int32)
    at_x = jnp.reshape(lax.axis_index("x"), (1,)).astype(jnp.int32)
    swap = [(0, 1), (1, 0)]

    spot = lax.broadcasted_iota(jnp.int32, (interface, 2 * n), 0)
    want = lax.broadcasted_iota(jnp.int32, (interface, 2 * n), 1)
    want = jnp.where(want < n, want * stride, (want - n) * stride + 1)
    face_map = jnp.dot(rows_map, (spot == want).astype(BF16), preferred_element_type=F32)
    west_high, west_low = halves(west)
    east_high, east_low = halves(east)
    face_low = face_map.astype(BF16)
    coupled = jnp.concatenate(
        [
            jnp.dot(face_low[:, :n], west_high, preferred_element_type=F32)
            + jnp.dot(face_low[:, :n], west_low, preferred_element_type=F32),
            jnp.dot(face_low[:, n:], east_high, preferred_element_type=F32)
            + jnp.dot(face_low[:, n:], east_low, preferred_element_type=F32),
        ],
        axis=1,
    ).astype(BF16)
    steps = coupled.reshape(nodes, stride, 2 * n)
    slices = jnp.concatenate([steps[:, 1, :n], steps[:, 0, :n], steps[:, 0, n:]], axis=0)
    slices = jnp.broadcast_to(slices, (peers,) + slices.shape)
    slices = lax.all_to_all(slices, GRP, 0, 0)
    maps = slices.reshape(peers, 3, nodes, n).transpose(1, 0, 2, 3).reshape(3 * n, n)
    rows = rows_map.reshape(nodes, stride, interface)
    rows = jnp.concatenate([rows[:, 1], rows[:, 0]], axis=0)
    face_rows = rows.reshape(2 * nodes, peers, width).transpose(1, 0, 2)
    face_rows = lax.all_to_all(face_rows, GRP, 0, 0)

    owner = nodes_of // width
    pos = ((owner % nc) ^ side) * half + (owner // nc) * width + nodes_of % width
    keep, send = call(
        spread_rows,
        (jax.ShapeDtypeStruct((half, columns), BF16),) * 2,
        [pltpu.VMEM((leaf_nodes, columns), F32), pltpu.VMEM((interface, columns), F32)],
        1,
        (2 * leaf_nodes * leaf_nodes * columns, 6 * leaf_nodes * leaf_nodes),
        pos,
        local_map,
        local_load,
    )
    maps, send = lax.optimization_barrier((maps, send))
    run_maps = lax.all_gather(maps, "y")
    got = lax.ppermute(send, "c", swap)
    paired = (keep.astype(F32) + got.astype(F32)).astype(BF16)
    parts = lax.all_to_all(paired.reshape(nz, width, columns), "z", 0, 0)
    loads, faces = call(
        face_parts,
        (
            jax.ShapeDtypeStruct((nz, width, columns), BF16),
            jax.ShapeDtypeStruct((peers, part, 2 * n), BF16),
        ),
        [pltpu.VMEM((2 * n, width), BF16)],
        0,
        (4 * n * width * columns, 4 * n * width),
        parts,
        face_rows,
    )
    faces = lax.all_to_all(faces, GRP, 0, 0)
    line = call(
        face_sum,
        jax.ShapeDtypeStruct((ny, part, 2 * n), BF16),
        [],
        0,
        (1000, 4 * n * columns),
        faces,
    )

    joined, own_maps = call(
        block_maps,
        (jax.ShapeDtypeStruct((3 * n, n), BF16), jax.ShapeDtypeStruct((3 * n, n), BF16)),
        [
            pltpu.VMEM((n, n), F32),
            pltpu.VMEM((n, 2 * n), F32),
            pltpu.VMEM((ny, n, n), F32),
        ],
        1,
        (16 * ny * n**3, 6 * ny * n * n),
        at_y,
        run_maps,
    )
    all_joined = lax.all_gather(joined, "x")

    line = moved(line, "y")
    ends, own_values = call(
        block_values,
        (
            jax.ShapeDtypeStruct((nx, part, 2 * n), BF16),
            jax.ShapeDtypeStruct((part, 2 * n), F32),
        ),
        [],
        1,
        (12 * ny * n * n * 16, 6 * ny * n * n),
        at_y,
        line,
        run_maps,
    )
    ends = moved(ends, "x")
    loads, ends = lax.optimization_barrier((loads, ends))
    loads_own = moved(loads, "z").reshape(half, columns)
    loads_other = lax.ppermute(loads_own, "c", swap)
    initial = call(
        functools.partial(first_rows, width=width),
        jax.ShapeDtypeStruct((width, columns), F32),
        [],
        1,
        (2 * width * interface * columns, 2 * width * interface),
        core,
        rows_map,
        loads_own,
        loads_other,
    )
    met = call(
        meet_values,
        jax.ShapeDtypeStruct((peers, part, 2 * n), BF16),
        [pltpu.VMEM((part, 2 * n), F32)],
        1,
        (12 * nx * n * n * 16, 6 * nx * n * n),
        at_x,
        ends,
        all_joined,
        own_maps,
        own_values,
    )
    met = lax.all_to_all(met, GRP, 0, 0).reshape(columns, 2 * n)

    final = initial + lax.dot_general(coupled, met, NT, preferred_element_type=F32)
    final = jnp.broadcast_to(final.astype(BF16), (nz, width, columns))
    final_own = lax.all_to_all(final, "z", 0, 0).reshape(half, columns)
    final_other = lax.ppermute(final_own, "c", swap)
    result = call(
        leaf_result,
        jax.ShapeDtypeStruct((leaf_nodes, columns), BF16),
        [pltpu.VMEM((interface, columns), F32), pltpu.VMEM((leaf_nodes, columns), F32)],
        1,
        (2 * leaf_nodes * leaf_nodes * columns, 2 * leaf_nodes * leaf_nodes),
        pos,
        final_own,
        final_other,
        local_map,
        local_load,
    )
    return result[None, None]


SPLITS = {(16, 32): (8, 2, 4, 8)}


def solution(mesh):
    shape = SPLITS.get(tuple(mesh.devices.shape), (2, 2, 2, 2))
    split = Mesh(mesh.devices.reshape(shape), ("z", "c", "x", "y"))
    grp, dom = ("z", "c"), ("x", "y")
    return jax.shard_map(
        on_device,
        mesh=split,
        in_specs=(
            P(dom, grp, None, None),
            P(dom, grp, None, None),
            P(dom, grp, None),
            P(dom, grp, None),
            P(dom, None, None),
            P(dom, None, None),
        ),
        out_specs=P(dom, grp, None, None),
        check_vma=False,
    )
```

```python
import functools

import jax
import jax.numpy as jnp
from jax import lax
from jax.experimental import pallas as pl
from jax.experimental.pallas import tpu as pltpu
from jax.sharding import Mesh
from jax.sharding import PartitionSpec as P


F32 = jnp.float32
BF16 = jnp.bfloat16
GRP = ("z", "c")
NT = (((1,), (1,)), ((), ()))
VM = pl.BlockSpec(memory_space=pltpu.VMEM)
SM = pl.BlockSpec(memory_space=pltpu.SMEM)
PARAMS = pltpu.CompilerParams(vmem_limit_bytes=16 * 1024 * 1024)


def call(kernel, outs, scratch, smem, cost, *args):
    specs = [SM] * smem + [VM] * (len(args) - smem)
    flops, moved = cost
    return pl.pallas_call(
        kernel,
        out_shape=outs,
        in_specs=specs,
        out_specs=jax.tree.map(lambda _: VM, outs),
        scratch_shapes=scratch,
        compiler_params=PARAMS,
        cost_estimate=pl.CostEstimate(flops=flops, bytes_accessed=moved, transcendentals=0),
    )(*args)


def ring(size, step):
    return [(i, (i + step) % size) for i in range(size)]


def moved(value, axis):
    return lax.all_to_all(value, axis, 0, 0)


def spread_rows(pos, map_ref, load_ref, keep_ref, send_ref, contrib, rows):
    contrib[...] = (
        jnp.dot(map_ref[...], load_ref[...], preferred_element_type=F32).astype(BF16).astype(F32)
    )
    rows[...] = jnp.zeros_like(rows)
    count = contrib.shape[0]
    unroll = 16

    def some(turn, carry):
        base = pl.multiple_of(turn * unroll, unroll)
        for k in range(unroll):
            rows[pl.ds(pos[base + k], 1), :] = contrib[pl.ds(base + k, 1), :]
        return carry

    lax.fori_loop(0, count // unroll, some, 0)
    half = keep_ref.shape[0]
    keep_ref[...] = rows[:half].astype(BF16)
    send_ref[...] = rows[half:].astype(BF16)


def sort_maps(core, got_ref, maps_ref, half_ref):
    peers, _, n = got_ref.shape
    nodes = n // peers
    for g in range(peers):
        for k in range(3):
            maps_ref[k * n + g * nodes : k * n + (g + 1) * nodes] = got_ref[
                g, k * nodes : (k + 1) * nodes
            ]
    rows = half_ref.shape[0]
    half_ref[...] = maps_ref[pl.ds(pl.multiple_of(core[0] * rows, rows), rows), :]


def face_parts(parts_ref, rows_ref, loads_ref, out_ref, order):
    total = parts_ref[0].astype(F32)
    for z in range(1, parts_ref.shape[0]):
        total = total + parts_ref[z].astype(F32)
    loads = total.astype(BF16)
    loads_ref[...] = loads
    peers, five, _ = rows_ref.shape
    nodes = five // 5
    for g in range(peers):
        order[g * nodes : (g + 1) * nodes] = rows_ref[g, 3 * nodes : 4 * nodes]
        order[(peers + g) * nodes : (peers + g + 1) * nodes] = rows_ref[g, 4 * nodes : five]
    lines = lax.dot_general(total.T.astype(BF16), order[...], NT, preferred_element_type=F32)
    part = out_ref.shape[1]
    for g in range(peers):
        out_ref[g] = lines[g * part : (g + 1) * part].astype(BF16)


def face_sum(got_ref, out_ref):
    total = got_ref[0].astype(F32)
    for g in range(1, got_ref.shape[0]):
        total = total + got_ref[g].astype(F32)
    line = total.astype(BF16)
    for y in range(out_ref.shape[0]):
        out_ref[y] = line


def first_rows(place, map_ref, own_ref, other_ref, initial_ref, *, width, masks):
    side, here = place[0], place[1]
    total = None
    for slot, mask in enumerate(masks):
        pair = 2 * (here ^ mask)
        mine = pl.ds(pl.multiple_of((pair + side) * width, width), width)
        theirs = pl.ds(pl.multiple_of((pair + 1 - side) * width, width), width)
        block = slice(slot * width, (slot + 1) * width)
        both = jnp.dot(map_ref[:, mine], own_ref[block], preferred_element_type=F32) + jnp.dot(
            map_ref[:, theirs], other_ref[block], preferred_element_type=F32
        )
        total = both if total is None else total + both
    initial_ref[...] = total


def lay_halves(target, side, slot, mine, other):
    rows = mine.shape[0]
    target[slot, pl.ds(pl.multiple_of(side * rows, rows), rows), :] = mine
    target[slot, pl.ds(pl.multiple_of((1 - side) * rows, rows), rows), :] = other


def halves(value):
    high = value.astype(BF16)
    low = (value - high.astype(F32)).astype(BF16)
    return high, low


def exact_right(left, value):
    high, low = halves(value)
    return jnp.dot(left, high, preferred_element_type=F32) + jnp.dot(
        left, low, preferred_element_type=F32
    )


def exact_rows(value, right):
    rows = value.shape[0]
    high, low = halves(value)
    both = lax.dot_general(
        jnp.concatenate([high, low], axis=0), right, NT, preferred_element_type=F32
    )
    return both[:rows] + both[rows:]


def block_maps(place, own_maps_ref, *refs, steps):
    mine, others = refs[: len(steps)], refs[len(steps) : -7]
    maps_ref, joined_ref, half_ref, own_ref, state, right, through = refs[-7:]
    count = maps_ref.shape[0]
    n = maps_ref.shape[2]
    here, side = place[0], place[1]
    maps_ref[here] = own_maps_ref[...]
    rows = half_ref.shape[0]
    pieces = [o[k * rows : (k + 1) * rows] for o in others for k in range(o.shape[0] // rows)]
    for step, one, other in zip(steps, mine, pieces, strict=True):
        lay_halves(maps_ref, side, lax.rem(here + step + count, count), one[...], other)
    unit = (
        lax.broadcasted_iota(jnp.int32, (n, n), 0) == lax.broadcasted_iota(jnp.int32, (n, n), 1)
    ).astype(F32)
    state[...] = unit

    def onward(j, carry):
        value = state[...]

        @pl.when(j == here)
        def _():
            own_ref[0:n] = value.astype(own_ref.dtype)

        both = exact_right(maps_ref[j, 0 : 2 * n, :], value)
        state[...] = both[:n]
        through[j] = both[n:]
        return carry

    lax.fori_loop(0, count, onward, 0)
    joined_ref[0:n] = state[...].astype(BF16)
    right[:, 0:n] = unit
    right[:, n : 2 * n] = jnp.zeros((n, n), F32)

    def back(turn, carry):
        j = count - 1 - turn
        value = right[...]

        @pl.when(j == here)
        def _():
            own_ref[n : 2 * n] = value[:, 0:n].astype(own_ref.dtype)
            own_ref[2 * n : 3 * n] = value[:, n : 2 * n].astype(own_ref.dtype)

        both = exact_right(maps_ref[j, 2 * n : 3 * n, :], value)
        right[:, 0:n] = both[:, 0:n]
        right[:, n : 2 * n] = both[:, n : 2 * n] + through[j]
        return carry

    lax.fori_loop(0, count, back, 0)
    joined_ref[n : 2 * n] = right[:, 0:n].astype(BF16)
    joined_ref[2 * n : 3 * n] = right[:, n : 2 * n].astype(BF16)
    half_ref[...] = joined_ref[pl.ds(pl.multiple_of(side * rows, rows), rows), :]


def block_values(place, faces_ref, maps_ref, ends_ref, own_ref):
    count, part, _ = faces_ref.shape
    n = maps_ref.shape[2]
    here = place[0]
    value = jnp.zeros((part, n), F32)
    sources = []
    for j in range(count):

        @pl.when(here == j)
        def _(value=value):
            own_ref[:, 0:n] = value

        both = exact_rows(value, maps_ref[j, 0 : 2 * n, :]) if j else None
        given = faces_ref[j].astype(F32)
        if j:
            value = given[:, 0:n] + both[:, 0:n]
            sources.append(given[:, n : 2 * n] + both[:, n : 2 * n])
        else:
            value = given[:, 0:n]
            sources.append(given[:, n : 2 * n])
    east = value
    value = jnp.zeros((part, n), F32)
    for j in range(count - 1, -1, -1):

        @pl.when(here == j)
        def _(value=value):
            own_ref[:, n : 2 * n] = value

        value = sources[j] + (
            exact_rows(value, maps_ref[j, 2 * n : 3 * n, :]) if j < count - 1 else 0.0
        )
    ends = jnp.concatenate([east, value], axis=1).astype(BF16)
    for x in range(ends_ref.shape[0]):
        ends_ref[x] = ends


def meet_values(place, ends_ref, own_joined_ref, *refs, steps):
    mine = refs[: len(steps)]
    others, maps_ref, own_ref, out_ref, entering, joined_ref = refs[len(steps) :]
    count, part, _ = ends_ref.shape
    n = joined_ref.shape[2]
    here, side = place[0], place[1]
    joined_ref[here] = own_joined_ref[...]
    rows = mine[0].shape[0]
    for k, step in enumerate(steps):
        other = others[k * rows : (k + 1) * rows]
        lay_halves(joined_ref, side, lax.rem(here + step + count, count), mine[k][...], other)
    east = jnp.zeros((part, n), F32)
    sources = []
    for b in range(count):

        @pl.when(here == b)
        def _(east=east):
            entering[:, 0:n] = east

        end = ends_ref[b].astype(F32)
        source = end[:, n : 2 * n]
        if b:
            source = source + exact_rows(east, joined_ref[b, 2 * n : 3 * n, :])
        sources.append(source)
        east = end[:, 0:n] + (exact_rows(east, joined_ref[b, 0:n, :]) if b else 0.0)
    west = jnp.zeros((part, n), F32)
    for b in range(count - 1, -1, -1):

        @pl.when(here == b)
        def _(west=west):
            entering[:, n : 2 * n] = west

        west = sources[b] + (
            exact_rows(west, joined_ref[b, n : 2 * n, :]) if b < count - 1 else 0.0
        )
    east = entering[:, 0:n]
    west = entering[:, n : 2 * n]
    own = own_ref[...]
    met_east = own[:, 0:n] + exact_rows(east, maps_ref[0:n])
    met_west = (
        own[:, n : 2 * n]
        + exact_rows(west, maps_ref[n : 2 * n])
        + exact_rows(east, maps_ref[2 * n : 3 * n])
    )
    met = jnp.concatenate([met_east, met_west], axis=1).astype(BF16)
    for g in range(out_ref.shape[0]):
        out_ref[g] = met


def leaf_result(pos, own_ref, other_ref, map_ref, load_ref, out_ref, rows, picked):
    half = own_ref.shape[0]
    rows[0:half] = own_ref[...].astype(F32)
    rows[half : 2 * half] = other_ref[...].astype(F32)
    count = picked.shape[0]
    unroll = 16

    def some(turn, carry):
        base = pl.multiple_of(turn * unroll, unroll)
        for k in range(unroll):
            picked[pl.ds(base + k, 1), :] = rows[pl.ds(pos[base + k], 1), :]
        return carry

    lax.fori_loop(0, count // unroll, some, 0)
    turned = picked[...].T.astype(BF16)
    result = jnp.dot(turned, map_ref[...], preferred_element_type=F32)
    out_ref[...] = (result.T + load_ref[...].astype(F32)).astype(BF16)


def on_device(leaf_load, leaf_map, group_map, node_index, west_coupling, east_coupling):
    local_map, local_load, nodes_of = leaf_map[0, 0], leaf_load[0, 0], node_index[0, 0]
    rows_map, west, east = group_map[0], west_coupling[0], east_coupling[0]
    nz, nc = lax.axis_size("z"), lax.axis_size("c")
    nx, ny = lax.axis_size("x"), lax.axis_size("y")
    peers = nz * nc
    leaf_nodes, columns = local_load.shape
    width, interface = rows_map.shape
    n = west.shape[0]
    stride = interface // n
    nodes = n // peers
    part = columns // peers
    half = interface // nc
    side = lax.axis_index("c")
    core = side.astype(jnp.int32)
    at_y = jnp.stack([lax.axis_index("y").astype(jnp.int32), core])
    at_x = jnp.stack([lax.axis_index("x").astype(jnp.int32), core])
    at_z = jnp.stack([core, lax.axis_index("z").astype(jnp.int32)])
    core = core.reshape((1,))
    swap = [(0, 1), (1, 0)]

    spot = lax.broadcasted_iota(jnp.int32, (interface, 2 * n), 0)
    want = lax.broadcasted_iota(jnp.int32, (interface, 2 * n), 1)
    want = jnp.where(want < n, want * stride, (want - n) * stride + 1)
    face_map = jnp.dot(rows_map, (spot == want).astype(BF16), preferred_element_type=F32)
    west_high, west_low = halves(west)
    east_high, east_low = halves(east)
    face_low = face_map.astype(BF16)
    coupled = jnp.concatenate(
        [
            jnp.dot(face_low[:, :n], west_high, preferred_element_type=F32)
            + jnp.dot(face_low[:, :n], west_low, preferred_element_type=F32),
            jnp.dot(face_low[:, n:], east_high, preferred_element_type=F32)
            + jnp.dot(face_low[:, n:], east_low, preferred_element_type=F32),
        ],
        axis=1,
    ).astype(BF16)
    steps = coupled.reshape(nodes, stride, 2 * n)
    slices = jnp.concatenate([steps[:, 1, :n], steps[:, 0, :n], steps[:, 0, n:]], axis=0)
    slices = jnp.broadcast_to(slices, (peers,) + slices.shape)
    rows = rows_map.reshape(nodes, stride, interface)
    rows = jnp.concatenate([rows[:, 1], rows[:, 0]], axis=0)
    rows = rows.reshape(2 * nodes, peers, width).transpose(1, 0, 2)
    pieces = lax.all_to_all(jnp.concatenate([slices, rows], axis=1), GRP, 0, 0)

    owner = nodes_of // width
    pos = ((owner % nc) ^ side) * half + (owner // nc) * width + nodes_of % width
    keep, send = call(
        spread_rows,
        (jax.ShapeDtypeStruct((half, columns), BF16),) * 2,
        [pltpu.VMEM((leaf_nodes, columns), F32), pltpu.VMEM((interface, columns), F32)],
        1,
        (2 * leaf_nodes * leaf_nodes * columns, 6 * leaf_nodes * leaf_nodes),
        pos,
        local_map,
        local_load,
    )
    got = lax.ppermute(send, "c", swap)
    paired = (keep.astype(F32) + got.astype(F32)).astype(BF16)
    pieces, paired = lax.optimization_barrier((pieces, paired))
    maps, half_maps = call(
        sort_maps,
        (jax.ShapeDtypeStruct((3 * n, n), BF16), jax.ShapeDtypeStruct((3 * n // nc, n), BF16)),
        [],
        1,
        (1000, 16 * n * n),
        core,
        pieces,
    )

    y_steps, y_mine = [], []
    up = down = half_maps
    for k in range(1, ny // 2 + 1):
        up = lax.ppermute(up, "y", ring(ny, 1))
        y_steps.append(-k)
        y_mine.append(up)
        if k < ny - k:
            down = lax.ppermute(down, "y", ring(ny, -1))
            y_steps.append(k)
            y_mine.append(down)
    near = (len(y_mine) + 1) // 2
    y_others = [
        lax.ppermute(jnp.concatenate(part_of, axis=0), "c", swap)
        for part_of in (y_mine[:near], y_mine[near:])
        if part_of
    ]

    parts = lax.all_to_all(paired.reshape(nz, width, columns), "z", 0, 0)
    loads, faces = call(
        face_parts,
        (
            jax.ShapeDtypeStruct((width, columns), BF16),
            jax.ShapeDtypeStruct((peers, part, 2 * n), BF16),
        ),
        [pltpu.VMEM((2 * n, width), BF16)],
        0,
        (4 * n * width * columns, 4 * n * width),
        parts,
        pieces,
    )
    faces = lax.all_to_all(faces, GRP, 0, 0)
    line = call(
        face_sum,
        jax.ShapeDtypeStruct((ny, part, 2 * n), BF16),
        [],
        0,
        (1000, 4 * n * columns),
        faces,
    )

    run_maps, joined, half_joined, own_maps = call(
        functools.partial(block_maps, steps=tuple(y_steps)),
        (
            jax.ShapeDtypeStruct((ny, 3 * n, n), BF16),
            jax.ShapeDtypeStruct((3 * n, n), BF16),
            jax.ShapeDtypeStruct((3 * n // nc, n), BF16),
            jax.ShapeDtypeStruct((3 * n, n), BF16),
        ),
        [
            pltpu.VMEM((n, n), F32),
            pltpu.VMEM((n, 2 * n), F32),
            pltpu.VMEM((ny, n, n), F32),
        ],
        1,
        (16 * ny * n**3, 6 * ny * n * n),
        at_y,
        maps,
        *y_mine,
        *y_others,
    )
    x_steps = [-1] + ([1] if nx > 2 else []) + ([-2] if nx > 3 else [])
    x_mine = [lax.ppermute(half_joined, "x", ring(nx, -step)) for step in x_steps]
    x_others = lax.ppermute(jnp.concatenate(x_mine, axis=0), "c", swap)

    masks = [0]
    loads_own = loads
    far = nz // 2
    while far:
        met_loads = lax.ppermute(loads_own, "z", [(z, z ^ far) for z in range(nz)])
        loads_own = jnp.concatenate([loads_own, met_loads], axis=0)
        masks += [mask ^ far for mask in masks]
        far //= 2
    loads_other = lax.ppermute(loads_own, "c", swap)
    initial = call(
        functools.partial(first_rows, width=width, masks=tuple(masks)),
        jax.ShapeDtypeStruct((width, columns), F32),
        [],
        1,
        (2 * width * interface * columns, 2 * width * interface),
        at_z,
        rows_map,
        loads_own,
        loads_other,
    )

    line = moved(line, "y")
    ends, own_values = call(
        block_values,
        (
            jax.ShapeDtypeStruct((nx, part, 2 * n), BF16),
            jax.ShapeDtypeStruct((part, 2 * n), F32),
        ),
        [],
        1,
        (12 * ny * n * n * 16, 6 * ny * n * n),
        at_y,
        line,
        run_maps,
    )
    ends = moved(ends, "x")
    met = call(
        functools.partial(meet_values, steps=tuple(x_steps)),
        jax.ShapeDtypeStruct((peers, part, 2 * n), BF16),
        [pltpu.VMEM((part, 2 * n), F32), pltpu.VMEM((nx, 3 * n, n), BF16)],
        1,
        (12 * nx * n * n * 16, 6 * nx * n * n),
        at_x,
        ends,
        joined,
        *x_mine,
        x_others,
        own_maps,
        own_values,
    )
    met = lax.all_to_all(met, GRP, 0, 0).reshape(columns, 2 * n)

    final = initial + lax.dot_general(coupled, met, NT, preferred_element_type=F32)
    final = jnp.broadcast_to(final.astype(BF16), (nz, width, columns))
    final_own = lax.all_to_all(final, "z", 0, 0).reshape(half, columns)
    final_other = lax.ppermute(final_own, "c", swap)
    result = call(
        leaf_result,
        jax.ShapeDtypeStruct((leaf_nodes, columns), BF16),
        [pltpu.VMEM((interface, columns), F32), pltpu.VMEM((leaf_nodes, columns), F32)],
        1,
        (2 * leaf_nodes * leaf_nodes * columns, 2 * leaf_nodes * leaf_nodes),
        pos,
        final_own,
        final_other,
        local_map,
        local_load,
    )
    return result[None, None]


SPLITS = {(16, 32): (8, 2, 4, 8)}


def solution(mesh):
    shape = SPLITS.get(tuple(mesh.devices.shape), (2, 2, 2, 2))
    split = Mesh(mesh.devices.reshape(shape), ("z", "c", "x", "y"))
    grp, dom = ("z", "c"), ("x", "y")
    return jax.shard_map(
        on_device,
        mesh=split,
        in_specs=(
            P(dom, grp, None, None),
            P(dom, grp, None, None),
            P(dom, grp, None),
            P(dom, grp, None),
            P(dom, None, None),
            P(dom, None, None),
        ),
        out_specs=P(dom, grp, None, None),
        check_vma=False,
    )
```

```python
import functools

import jax
import jax.numpy as jnp
from jax import lax
from jax.experimental import pallas as pl
from jax.experimental.pallas import tpu as pltpu
from jax.sharding import Mesh
from jax.sharding import PartitionSpec as P


F32 = jnp.float32
BF16 = jnp.bfloat16
GRP = ("z", "c")
NT = (((1,), (1,)), ((), ()))
VM = pl.BlockSpec(memory_space=pltpu.VMEM)
SM = pl.BlockSpec(memory_space=pltpu.SMEM)
PARAMS = pltpu.CompilerParams(vmem_limit_bytes=16 * 1024 * 1024)


def call(kernel, name, outs, scratch, smem, cost, *args):
    specs = [SM] * smem + [VM] * (len(args) - smem)
    flops, moved = cost
    return pl.pallas_call(
        kernel,
        name=name,
        out_shape=outs,
        in_specs=specs,
        out_specs=jax.tree.map(lambda _: VM, outs),
        scratch_shapes=scratch,
        compiler_params=PARAMS,
        cost_estimate=pl.CostEstimate(flops=flops, bytes_accessed=moved, transcendentals=0),
    )(*args)


def spread_rows(pos, map_ref, load_ref, keep_ref, send_ref, contrib, rows):
    contrib[...] = (
        jnp.dot(map_ref[...], load_ref[...], preferred_element_type=F32).astype(BF16).astype(F32)
    )
    rows[...] = jnp.zeros_like(rows)
    count = contrib.shape[0]
    unroll = 16

    def some(turn, carry):
        base = pl.multiple_of(turn * unroll, unroll)
        for k in range(unroll):
            rows[pl.ds(pos[base + k], 1), :] = contrib[pl.ds(base + k, 1), :]
        return carry

    lax.fori_loop(0, count // unroll, some, 0)
    half = keep_ref.shape[0]
    keep_ref[...] = rows[:half].astype(BF16)
    send_ref[...] = rows[half:].astype(BF16)


def sort_maps(got_ref, maps_ref):
    peers, _, n = got_ref.shape
    nodes = n // peers
    for g in range(peers):
        for k in range(3):
            maps_ref[k * n + g * nodes : k * n + (g + 1) * nodes] = got_ref[
                g, k * nodes : (k + 1) * nodes
            ]


def face_parts(parts_ref, rows_ref, loads_ref, out_ref, order):
    total = parts_ref[0].astype(F32)
    for z in range(1, parts_ref.shape[0]):
        total = total + parts_ref[z].astype(F32)
    loads = total.astype(BF16)
    loads_ref[...] = loads
    peers, five, _ = rows_ref.shape
    nodes = five // 5
    for g in range(peers):
        order[g * nodes : (g + 1) * nodes] = rows_ref[g, 3 * nodes : 4 * nodes]
        order[(peers + g) * nodes : (peers + g + 1) * nodes] = rows_ref[g, 4 * nodes : five]
    lines = lax.dot_general(total.T.astype(BF16), order[...], NT, preferred_element_type=F32)
    part = out_ref.shape[1]
    for g in range(peers):
        out_ref[g] = lines[g * part : (g + 1) * part].astype(BF16)


def face_sum(got_ref, out_ref):
    total = got_ref[0].astype(F32)
    for g in range(1, got_ref.shape[0]):
        total = total + got_ref[g].astype(F32)
    line = total.astype(BF16)
    for y in range(out_ref.shape[0]):
        out_ref[y] = line


def halves(value):
    high = value.astype(BF16)
    low = (value - high.astype(F32)).astype(BF16)
    return high, low


def exact_right(left, value):
    high, low = halves(value)
    return jnp.dot(left, high, preferred_element_type=F32) + jnp.dot(
        left, low, preferred_element_type=F32
    )


def exact_rows(value, right):
    rows = value.shape[0]
    high, low = halves(value)
    both = lax.dot_general(
        jnp.concatenate([high, low], axis=0), right, NT, preferred_element_type=F32
    )
    return both[:rows] + both[rows:]


def run_block(place, faces_ref, maps_ref, ends_ref, own_maps_ref, own_ref, *scratch):
    state, right, through, given, sources = scratch
    count, part, _ = faces_ref.shape
    n = maps_ref.shape[2]
    here = place[0]
    unit = (
        lax.broadcasted_iota(jnp.int32, (n, n), 0) == lax.broadcasted_iota(jnp.int32, (n, n), 1)
    ).astype(F32)
    state[...] = unit
    right[:, 0:n] = unit
    right[:, n : 2 * n] = jnp.zeros((n, n), F32)
    given[...] = jnp.zeros_like(given)

    def onward(j, carry):
        value = state[...]
        east = given[:, 0:n]

        @pl.when(j == here)
        def _():
            own_maps_ref[0:n] = value.astype(BF16)
            own_ref[:, 0:n] = east

        maps = maps_ref[j, 0 : 2 * n, :]
        both = exact_right(maps, value)
        moved = faces_ref[j].astype(F32) + exact_rows(east, maps)
        state[...] = both[:n]
        through[j] = both[n:]
        given[:, 0:n] = moved[:, 0:n]
        sources[j] = moved[:, n : 2 * n]
        return carry

    lax.fori_loop(0, count, onward, 0)

    def back(turn, carry):
        j = count - 1 - turn
        value = right[...]
        west = given[:, n : 2 * n]

        @pl.when(j == here)
        def _():
            own_maps_ref[n : 2 * n] = value[:, 0:n].astype(BF16)
            own_maps_ref[2 * n : 3 * n] = value[:, n : 2 * n].astype(BF16)
            own_ref[:, n : 2 * n] = west

        maps = maps_ref[j, 2 * n : 3 * n, :]
        both = exact_right(maps, value)
        moved = sources[j] + exact_rows(west, maps)
        right[:, 0:n] = both[:, 0:n]
        right[:, n : 2 * n] = both[:, n : 2 * n] + through[j]
        given[:, n : 2 * n] = moved
        return carry

    lax.fori_loop(0, count, back, 0)
    ends = jnp.concatenate([given[:, 0:n], given[:, n : 2 * n]], axis=0).astype(BF16)
    for x in range(ends_ref.shape[0]):
        ends_ref[x, 0:n] = state[...].astype(BF16)
        ends_ref[x, n : 2 * n] = right[:, 0:n].astype(BF16)
        ends_ref[x, 2 * n : 3 * n] = right[:, n : 2 * n].astype(BF16)
        ends_ref[x, 3 * n : 3 * n + 2 * part] = ends


def meet_values(place, ends_ref, maps_ref, own_ref, out_ref, entering):
    count, _, n = ends_ref.shape
    part = own_ref.shape[0]
    here = place[0]
    east = jnp.zeros((part, n), F32)
    sources = []
    for b in range(count):

        @pl.when(here == b)
        def _(east=east):
            entering[:, 0:n] = east

        end = ends_ref[b, 3 * n : 3 * n + 2 * part].astype(F32)
        source = end[part : 2 * part]
        if b:
            source = source + exact_rows(east, ends_ref[b, 2 * n : 3 * n, :])
        sources.append(source)
        east = end[0:part] + (exact_rows(east, ends_ref[b, 0:n, :]) if b else 0.0)
    west = jnp.zeros((part, n), F32)
    for b in range(count - 1, -1, -1):

        @pl.when(here == b)
        def _(west=west):
            entering[:, n : 2 * n] = west

        west = sources[b] + (
            exact_rows(west, ends_ref[b, n : 2 * n, :]) if b < count - 1 else 0.0
        )
    east = entering[:, 0:n]
    west = entering[:, n : 2 * n]
    own = own_ref[...]
    met_east = own[:, 0:n] + exact_rows(east, maps_ref[0:n])
    met_west = (
        own[:, n : 2 * n]
        + exact_rows(west, maps_ref[n : 2 * n])
        + exact_rows(east, maps_ref[2 * n : 3 * n])
    )
    met = jnp.concatenate([met_east, met_west], axis=1).astype(BF16)
    for g in range(out_ref.shape[0]):
        out_ref[g] = met


def leaf_result(pos, own_ref, other_ref, map_ref, load_ref, out_ref, rows, picked):
    half = own_ref.shape[0]
    rows[0:half] = own_ref[...].astype(F32)
    rows[half : 2 * half] = other_ref[...].astype(F32)
    count = picked.shape[0]
    unroll = 16

    def some(turn, carry):
        base = pl.multiple_of(turn * unroll, unroll)
        for k in range(unroll):
            picked[pl.ds(base + k, 1), :] = rows[pl.ds(pos[base + k], 1), :]
        return carry

    lax.fori_loop(0, count // unroll, some, 0)
    turned = picked[...].T.astype(BF16)
    result = jnp.dot(turned, map_ref[...], preferred_element_type=F32)
    out_ref[...] = (result.T + load_ref[...].astype(F32)).astype(BF16)


def on_device(leaf_load, leaf_map, group_map, node_index, west_coupling, east_coupling):
    local_map, local_load, nodes_of = leaf_map[0, 0], leaf_load[0, 0], node_index[0, 0]
    rows_map, west, east = group_map[0], west_coupling[0], east_coupling[0]
    nz, nc = lax.axis_size("z"), lax.axis_size("c")
    nx, ny = lax.axis_size("x"), lax.axis_size("y")
    peers = nz * nc
    leaf_nodes, columns = local_load.shape
    width, interface = rows_map.shape
    n = west.shape[0]
    stride = interface // n
    nodes = n // peers
    part = columns // peers
    half = interface // nc
    side = lax.axis_index("c")
    at_y = jnp.reshape(lax.axis_index("y"), (1,)).astype(jnp.int32)
    at_x = jnp.reshape(lax.axis_index("x"), (1,)).astype(jnp.int32)
    swap = [(0, 1), (1, 0)]

    spot = lax.broadcasted_iota(jnp.int32, (interface, 2 * n), 0)
    want = lax.broadcasted_iota(jnp.int32, (interface, 2 * n), 1)
    want = jnp.where(want < n, want * stride, (want - n) * stride + 1)
    face_map = jnp.dot(rows_map, (spot == want).astype(BF16), preferred_element_type=F32)
    west_high, west_low = halves(west)
    east_high, east_low = halves(east)
    face_low = face_map.astype(BF16)
    coupled = jnp.concatenate(
        [
            jnp.dot(face_low[:, :n], west_high, preferred_element_type=F32)
            + jnp.dot(face_low[:, :n], west_low, preferred_element_type=F32),
            jnp.dot(face_low[:, n:], east_high, preferred_element_type=F32)
            + jnp.dot(face_low[:, n:], east_low, preferred_element_type=F32),
        ],
        axis=1,
    ).astype(BF16)
    steps = coupled.reshape(nodes, stride, 2 * n)
    slices = jnp.concatenate([steps[:, 1, :n], steps[:, 0, :n], steps[:, 0, n:]], axis=0)
    slices = jnp.broadcast_to(slices, (peers,) + slices.shape)
    rows = rows_map.reshape(nodes, stride, interface)
    rows = jnp.concatenate([rows[:, 1], rows[:, 0]], axis=0)
    rows = rows.reshape(2 * nodes, peers, width).transpose(1, 0, 2)
    pieces = lax.all_to_all(jnp.concatenate([slices, rows], axis=1), GRP, 0, 0)

    owner = nodes_of // width
    pos = ((owner % nc) ^ side) * half + (owner // nc) * width + nodes_of % width
    keep, send = call(
        spread_rows,
        "spread_rows",
        (jax.ShapeDtypeStruct((half, columns), BF16),) * 2,
        [pltpu.VMEM((leaf_nodes, columns), F32), pltpu.VMEM((interface, columns), F32)],
        1,
        (2 * leaf_nodes * leaf_nodes * columns, 6 * leaf_nodes * leaf_nodes),
        pos,
        local_map,
        local_load,
    )
    got = lax.ppermute(send, "c", swap)
    paired = (keep.astype(F32) + got.astype(F32)).astype(BF16)
    pieces, paired = lax.optimization_barrier((pieces, paired))
    maps = call(
        sort_maps,
        "sort_maps",
        jax.ShapeDtypeStruct((3 * n, n), BF16),
        [],
        0,
        (1000, 16 * n * n),
        pieces,
    )
    run_maps = lax.all_gather(maps, "y")

    parts = lax.all_to_all(paired.reshape(nz, width, columns), "z", 0, 0)
    loads, faces = call(
        face_parts,
        "face_parts",
        (
            jax.ShapeDtypeStruct((width, columns), BF16),
            jax.ShapeDtypeStruct((peers, part, 2 * n), BF16),
        ),
        [pltpu.VMEM((2 * n, width), BF16)],
        0,
        (4 * n * width * columns, 4 * n * width),
        parts,
        pieces,
    )
    faces = lax.all_to_all(faces, GRP, 0, 0)
    line = call(
        face_sum,
        "face_sum",
        jax.ShapeDtypeStruct((ny, part, 2 * n), BF16),
        [],
        0,
        (1000, 4 * n * columns),
        faces,
    )

    all_loads = lax.all_gather(loads, GRP, axis=0, tiled=True)

    line = lax.all_to_all(line, "y", 0, 0)
    ends, own_maps, own_values = call(
        run_block,
        "run_block",
        (
            jax.ShapeDtypeStruct((nx, 3 * n + 2 * part, n), BF16),
            jax.ShapeDtypeStruct((3 * n, n), BF16),
            jax.ShapeDtypeStruct((part, 2 * n), F32),
        ),
        [
            pltpu.VMEM((n, n), F32),
            pltpu.VMEM((n, 2 * n), F32),
            pltpu.VMEM((ny, n, n), F32),
            pltpu.VMEM((part, 2 * n), F32),
            pltpu.VMEM((ny, part, n), F32),
        ],
        1,
        (16 * ny * n**3, 6 * ny * n * n),
        at_y,
        line,
        run_maps,
    )
    ends = lax.all_to_all(ends, "x", 0, 0)
    met = call(
        meet_values,
        "meet_values",
        jax.ShapeDtypeStruct((peers, part, 2 * n), BF16),
        [pltpu.VMEM((part, 2 * n), F32)],
        1,
        (12 * nx * n * n * 16, 6 * nx * n * n),
        at_x,
        ends,
        own_maps,
        own_values,
    )
    met_blocks = lax.all_to_all(met, GRP, 0, 0)

    all_loads, _ = lax.optimization_barrier((all_loads, met))
    initial = jnp.dot(rows_map, all_loads, preferred_element_type=F32)
    met = met_blocks.reshape(columns, 2 * n)
    final = initial + lax.dot_general(coupled, met, NT, preferred_element_type=F32)
    final = jnp.broadcast_to(final.astype(BF16), (nz, width, columns))
    final_own = lax.all_to_all(final, "z", 0, 0).reshape(half, columns)
    final_other = lax.ppermute(final_own, "c", swap)
    result = call(
        leaf_result,
        "leaf_result",
        jax.ShapeDtypeStruct((leaf_nodes, columns), BF16),
        [pltpu.VMEM((interface, columns), F32), pltpu.VMEM((leaf_nodes, columns), F32)],
        1,
        (2 * leaf_nodes * leaf_nodes * columns, 2 * leaf_nodes * leaf_nodes),
        pos,
        final_own,
        final_other,
        local_map,
        local_load,
    )
    return result[None, None]


SPLITS = {(16, 32): (8, 2, 4, 8)}


def solution(mesh):
    shape = SPLITS.get(tuple(mesh.devices.shape), (2, 2, 2, 2))
    split = Mesh(mesh.devices.reshape(shape), ("z", "c", "x", "y"))
    grp, dom = ("z", "c"), ("x", "y")
    return jax.shard_map(
        on_device,
        mesh=split,
        in_specs=(
            P(dom, grp, None, None),
            P(dom, grp, None, None),
            P(dom, grp, None),
            P(dom, grp, None),
            P(dom, None, None),
            P(dom, None, None),
        ),
        out_specs=P(dom, grp, None, None),
        check_vma=False,
    )
```

```python
import functools

import jax
import jax.numpy as jnp
from jax import lax
from jax.experimental import pallas as pl
from jax.experimental.pallas import tpu as pltpu
from jax.sharding import Mesh
from jax.sharding import PartitionSpec as P

F32 = jnp.float32
BF16 = jnp.bfloat16
GRP = ("z", "c")
NT = (((1,), (1,)), ((), ()))
VM = pl.BlockSpec(memory_space=pltpu.VMEM)
SM = pl.BlockSpec(memory_space=pltpu.SMEM)
FAR = pl.BlockSpec(memory_space=pltpu.HBM)
PARAMS = pltpu.CompilerParams(vmem_limit_bytes=16 * 1024 * 1024)


def call(kernel, name, outs, scratch, smem, cost, *args, far=0):
    specs = [SM] * smem + [VM] * (len(args) - smem - far) + [FAR] * far
    flops, moved = cost
    return pl.pallas_call(
        kernel,
        name=name,
        out_shape=outs,
        in_specs=specs,
        out_specs=jax.tree.map(lambda _: VM, outs),
        scratch_shapes=scratch,
        compiler_params=PARAMS,
        cost_estimate=pl.CostEstimate(flops=flops, bytes_accessed=moved, transcendentals=0),
    )(*args)


def spread_rows(pos, map_ref, load_ref, keep_ref, send_ref, contrib, rows):
    contrib[...] = (
        jnp.dot(map_ref[...], load_ref[...], preferred_element_type=F32).astype(BF16).astype(F32)
    )
    rows[...] = jnp.zeros_like(rows)
    count = contrib.shape[0]
    unroll = 16

    def some(turn, carry):
        base = pl.multiple_of(turn * unroll, unroll)
        for k in range(unroll):
            rows[pl.ds(pos[base + k], 1), :] = contrib[pl.ds(base + k, 1), :]
        return carry

    lax.fori_loop(0, count // unroll, some, 0)
    half = keep_ref.shape[0]
    keep_ref[...] = rows[:half].astype(BF16)
    send_ref[...] = rows[half:].astype(BF16)


def first_pieces(map_ref, west_ref, east_ref, out_ref, rows, turned, *, stride):
    count = map_ref.shape[0] // stride
    for k in range(count):
        pair = map_ref[k * stride : (k + 1) * stride, :].astype(F32)
        rows[k : k + 1, :] = pair[0:1]
        rows[count + k : count + k + 1, :] = pair[1:2]
    turned[...] = rows[...].T
    n = west_ref.shape[0]

    def coupled(at, coupling):
        picked = turned[pl.ds(at, n, stride=stride), :].T.astype(BF16)
        high, low = halves(coupling)
        return jnp.dot(picked, high, preferred_element_type=F32) + jnp.dot(
            picked, low, preferred_element_type=F32
        )

    by_west = coupled(0, west_ref[...]).astype(BF16)
    by_east = coupled(1, east_ref[...]).astype(BF16)
    width = out_ref.shape[2]
    for g in range(out_ref.shape[0]):
        block = slice(g * width, (g + 1) * width)
        out_ref[g, 0:count] = by_west[count:]
        out_ref[g, count : 2 * count] = by_west[:count]
        out_ref[g, 2 * count : 3 * count] = by_east[:count]
        out_ref[g, 3 * count : 4 * count] = rows[count:, block].astype(BF16)
        out_ref[g, 4 * count : 5 * count] = rows[:count, block].astype(BF16)


def lay_halves(target, slot, side, mine, other):
    rows = mine.shape[0]
    target[slot, pl.ds(pl.multiple_of(side * rows, rows), rows), :] = mine
    target[slot, pl.ds(pl.multiple_of((1 - side) * rows, rows), rows), :] = other


def sort_maps(got_ref, maps_ref):
    peers, _, n = got_ref.shape
    nodes = n // peers
    for g in range(peers):
        for k in range(3):
            maps_ref[k * n + g * nodes : k * n + (g + 1) * nodes] = got_ref[
                g, k * nodes : (k + 1) * nodes
            ]


def face_parts(parts_ref, rows_ref, loads_ref, out_ref, order):
    total = parts_ref[0].astype(F32)
    for z in range(1, parts_ref.shape[0]):
        total = total + parts_ref[z].astype(F32)
    loads = total.astype(BF16)
    loads_ref[...] = loads
    peers, five, _ = rows_ref.shape
    nodes = five // 5
    for g in range(peers):
        order[g * nodes : (g + 1) * nodes] = rows_ref[g, 3 * nodes : 4 * nodes]
        order[(peers + g) * nodes : (peers + g + 1) * nodes] = rows_ref[g, 4 * nodes : five]
    lines = lax.dot_general(total.T.astype(BF16), order[...], NT, preferred_element_type=F32)
    part = out_ref.shape[1]
    for g in range(peers):
        out_ref[g] = lines[g * part : (g + 1) * part].astype(BF16)


def face_sum(got_ref, out_ref):
    total = got_ref[0].astype(F32)
    for g in range(1, got_ref.shape[0]):
        total = total + got_ref[g].astype(F32)
    line = total.astype(BF16)
    for y in range(out_ref.shape[0]):
        out_ref[y] = line


def halves(value):
    high = value.astype(BF16)
    low = (value - high.astype(F32)).astype(BF16)
    return high, low


def exact_right(left, value):
    high, low = halves(value)
    return jnp.dot(left, high, preferred_element_type=F32) + jnp.dot(
        left, low, preferred_element_type=F32
    )


def exact_rows(value, right):
    rows = value.shape[0]
    high, low = halves(value)
    both = lax.dot_general(
        jnp.concatenate([high, low], axis=0), right, NT, preferred_element_type=F32
    )
    return both[:rows] + both[rows:]


def run_block(place, faces_ref, far_maps_ref, ends_ref, own_maps_ref, own_ref, *scratch):
    state, right, through, given, sources, joined, maps_ref, done = scratch
    count, part, _ = faces_ref.shape
    n = maps_ref.shape[2]
    here, side = place[0], place[1]

    def fetch(j):
        return pltpu.make_async_copy(far_maps_ref.at[j], maps_ref.at[j], done.at[j])

    for j in range(count):
        fetch(j).start()
    unit = (
        lax.broadcasted_iota(jnp.int32, (n, n), 0) == lax.broadcasted_iota(jnp.int32, (n, n), 1)
    ).astype(F32)
    state[...] = unit
    right[:, 0:n] = unit
    right[:, n : 2 * n] = jnp.zeros((n, n), F32)
    given[...] = jnp.zeros_like(given)

    def onward(j, carry):
        value = state[...]
        east = given[:, 0:n]

        @pl.when(j == here)
        def _():
            own_maps_ref[0:n] = value.astype(BF16)
            own_ref[:, 0:n] = east

        fetch(j).wait()
        maps = maps_ref[j, 0 : 2 * n, :]
        both = exact_right(maps, value)
        moved = faces_ref[j].astype(F32) + exact_rows(east, maps)
        state[...] = both[:n]
        through[j] = both[n:]
        given[:, 0:n] = moved[:, 0:n]
        sources[j] = moved[:, n : 2 * n]
        return carry

    lax.fori_loop(0, count, onward, 0)

    def back(turn, carry):
        j = count - 1 - turn
        value = right[...]
        west = given[:, n : 2 * n]

        @pl.when(j == here)
        def _():
            own_maps_ref[n : 2 * n] = value[:, 0:n].astype(BF16)
            own_maps_ref[2 * n : 3 * n] = value[:, n : 2 * n].astype(BF16)
            own_ref[:, n : 2 * n] = west

        maps = maps_ref[j, 2 * n : 3 * n, :]
        both = exact_right(maps, value)
        moved = sources[j] + exact_rows(west, maps)
        right[:, 0:n] = both[:, 0:n]
        right[:, n : 2 * n] = both[:, n : 2 * n] + through[j]
        given[:, n : 2 * n] = moved
        return carry

    lax.fori_loop(0, count, back, 0)
    ends = jnp.concatenate([given[:, 0:n], given[:, n : 2 * n]], axis=0).astype(BF16)
    joined[0:n] = state[...].astype(BF16)
    joined[n : 2 * n] = right[:, 0:n].astype(BF16)
    joined[2 * n : 3 * n] = right[:, n : 2 * n].astype(BF16)
    rows = ends_ref.shape[1] - 2 * part
    half = joined[pl.ds(pl.multiple_of(side * rows, rows), rows), :]
    for x in range(ends_ref.shape[0]):
        ends_ref[x, 0:rows] = half
        ends_ref[x, rows : rows + 2 * part] = ends


def meet_values(place, ends_ref, other_ref, maps_ref, own_ref, out_ref, entering, joined_ref):
    count, _, n = ends_ref.shape
    part = own_ref.shape[0]
    here, side = place[0], place[1]
    rows = ends_ref.shape[1] - 2 * part
    for b in range(count):
        lay_halves(joined_ref, b, side, ends_ref[b, 0:rows], other_ref[b, 0:rows])
    east = jnp.zeros((part, n), F32)
    sources = []
    for b in range(count):

        @pl.when(here == b)
        def _(east=east):
            entering[:, 0:n] = east

        end = ends_ref[b, rows : rows + 2 * part].astype(F32)
        source = end[part : 2 * part]
        if b:
            source = source + exact_rows(east, joined_ref[b, 2 * n : 3 * n, :])
        sources.append(source)
        east = end[0:part] + (exact_rows(east, joined_ref[b, 0:n, :]) if b else 0.0)
    west = jnp.zeros((part, n), F32)
    for b in range(count - 1, -1, -1):

        @pl.when(here == b)
        def _(west=west):
            entering[:, n : 2 * n] = west

        west = sources[b] + (
            exact_rows(west, joined_ref[b, n : 2 * n, :]) if b < count - 1 else 0.0
        )
    east = entering[:, 0:n]
    west = entering[:, n : 2 * n]
    own = own_ref[...]
    met_east = own[:, 0:n] + exact_rows(east, maps_ref[0:n])
    met_west = (
        own[:, n : 2 * n]
        + exact_rows(west, maps_ref[n : 2 * n])
        + exact_rows(east, maps_ref[2 * n : 3 * n])
    )
    met = jnp.concatenate([met_east, met_west], axis=1).astype(BF16)
    for g in range(out_ref.shape[0]):
        out_ref[g] = met


def leaf_result(pos, own_ref, other_ref, map_ref, load_ref, out_ref, rows, picked):
    half = own_ref.shape[0]
    rows[0:half] = own_ref[...].astype(F32)
    rows[half : 2 * half] = other_ref[...].astype(F32)
    count = picked.shape[0]
    unroll = 16

    def some(turn, carry):
        base = pl.multiple_of(turn * unroll, unroll)
        for k in range(unroll):
            picked[pl.ds(base + k, 1), :] = rows[pl.ds(pos[base + k], 1), :]
        return carry

    lax.fori_loop(0, count // unroll, some, 0)
    turned = picked[...].T.astype(BF16)
    result = jnp.dot(turned, map_ref[...], preferred_element_type=F32)
    out_ref[...] = (result.T + load_ref[...].astype(F32)).astype(BF16)


def on_device(leaf_load, leaf_map, group_map, node_index, west_coupling, east_coupling):
    local_map, local_load, nodes_of = leaf_map[0, 0], leaf_load[0, 0], node_index[0, 0]
    rows_map, west, east = group_map[0], west_coupling[0], east_coupling[0]
    nz, nc = lax.axis_size("z"), lax.axis_size("c")
    nx, ny = lax.axis_size("x"), lax.axis_size("y")
    peers = nz * nc
    leaf_nodes, columns = local_load.shape
    width, interface = rows_map.shape
    n = west.shape[0]
    stride = interface // n
    nodes = n // peers
    part = columns // peers
    half = interface // nc
    side = lax.axis_index("c")
    core = side.astype(jnp.int32)
    at_y = jnp.stack([lax.axis_index("y").astype(jnp.int32), core])
    at_x = jnp.stack([lax.axis_index("x").astype(jnp.int32), core])
    swap = [(0, 1), (1, 0)]

    pieces = call(
        functools.partial(first_pieces, stride=stride),
        "first_pieces",
        jax.ShapeDtypeStruct((peers, 5 * nodes, width), BF16),
        [pltpu.VMEM((2 * nodes, interface), F32), pltpu.VMEM((interface, 2 * nodes), F32)],
        0,
        (8 * nodes * n * n, 2 * width * interface),
        rows_map,
        west,
        east,
    )
    pieces = lax.all_to_all(pieces, GRP, 0, 0)

    owner = nodes_of // width
    pos = ((owner % nc) ^ side) * half + (owner // nc) * width + nodes_of % width
    keep, send = call(
        spread_rows,
        "spread_rows",
        (jax.ShapeDtypeStruct((half, columns), BF16),) * 2,
        [pltpu.VMEM((leaf_nodes, columns), F32), pltpu.VMEM((interface, columns), F32)],
        1,
        (2 * leaf_nodes * leaf_nodes * columns, 6 * leaf_nodes * leaf_nodes),
        pos,
        local_map,
        local_load,
    )
    got = lax.ppermute(send, "c", swap)
    paired = (keep.astype(F32) + got.astype(F32)).astype(BF16)
    pieces, paired = lax.optimization_barrier((pieces, paired))
    maps = call(
        sort_maps,
        "sort_maps",
        jax.ShapeDtypeStruct((3 * n, n), BF16),
        [],
        0,
        (1000, 16 * n * n),
        pieces,
    )
    run_maps = lax.all_gather(maps, "y")

    parts = lax.all_to_all(paired.reshape(nz, width, columns), "z", 0, 0)
    late_map, _ = lax.optimization_barrier((rows_map, maps))
    spot = lax.broadcasted_iota(jnp.int32, (interface, 2 * n), 0)
    want = lax.broadcasted_iota(jnp.int32, (interface, 2 * n), 1)
    want = jnp.where(want < n, want * stride, (want - n) * stride + 1)
    face_map = jnp.dot(late_map, (spot == want).astype(BF16), preferred_element_type=F32)
    face_map = face_map.astype(BF16)
    west_high, west_low = halves(west)
    east_high, east_low = halves(east)
    coupled = jnp.concatenate(
        [
            jnp.dot(face_map[:, :n], west_high, preferred_element_type=F32)
            + jnp.dot(face_map[:, :n], west_low, preferred_element_type=F32),
            jnp.dot(face_map[:, n:], east_high, preferred_element_type=F32)
            + jnp.dot(face_map[:, n:], east_low, preferred_element_type=F32),
        ],
        axis=1,
    ).astype(BF16)

    loads, faces = call(
        face_parts,
        "face_parts",
        (
            jax.ShapeDtypeStruct((width, columns), BF16),
            jax.ShapeDtypeStruct((peers, part, 2 * n), BF16),
        ),
        [pltpu.VMEM((2 * n, width), BF16)],
        0,
        (4 * n * width * columns, 4 * n * width),
        parts,
        pieces,
    )
    faces = lax.all_to_all(faces, GRP, 0, 0)
    line = call(
        face_sum,
        "face_sum",
        jax.ShapeDtypeStruct((ny, part, 2 * n), BF16),
        [],
        0,
        (1000, 4 * n * columns),
        faces,
    )

    all_loads = lax.all_gather(loads, GRP, axis=0, tiled=True)

    line = lax.all_to_all(line, "y", 0, 0)
    ends, own_maps, own_values = call(
        run_block,
        "run_block",
        (
            jax.ShapeDtypeStruct((nx, 3 * n // nc + 2 * part, n), BF16),
            jax.ShapeDtypeStruct((3 * n, n), BF16),
            jax.ShapeDtypeStruct((part, 2 * n), F32),
        ),
        [
            pltpu.VMEM((n, n), F32),
            pltpu.VMEM((n, 2 * n), F32),
            pltpu.VMEM((ny, n, n), F32),
            pltpu.VMEM((part, 2 * n), F32),
            pltpu.VMEM((ny, part, n), F32),
            pltpu.VMEM((3 * n, n), BF16),
            pltpu.VMEM((ny, 3 * n, n), BF16),
            pltpu.SemaphoreType.DMA((ny,)),
        ],
        1,
        (16 * ny * n**3, 6 * ny * n * n),
        at_y,
        line,
        run_maps,
        far=1,
    )
    ends = lax.all_to_all(ends, "x", 0, 0)
    other_ends = lax.ppermute(ends, "c", swap)
    met = call(
        meet_values,
        "meet_values",
        jax.ShapeDtypeStruct((peers, part, 2 * n), BF16),
        [pltpu.VMEM((part, 2 * n), F32), pltpu.VMEM((nx, 3 * n, n), BF16)],
        1,
        (12 * nx * n * n * 16, 6 * nx * n * n),
        at_x,
        ends,
        other_ends,
        own_maps,
        own_values,
    )
    met_blocks = lax.all_to_all(met, GRP, 0, 0)

    all_loads, _ = lax.optimization_barrier((all_loads, met))
    initial = jnp.dot(rows_map, all_loads, preferred_element_type=F32)
    met = met_blocks.reshape(columns, 2 * n)
    final = initial + lax.dot_general(coupled, met, NT, preferred_element_type=F32)
    final = jnp.broadcast_to(final.astype(BF16), (nz, width, columns))
    final_own = lax.all_to_all(final, "z", 0, 0).reshape(half, columns)
    final_other = lax.ppermute(final_own, "c", swap)
    result = call(
        leaf_result,
        "leaf_result",
        jax.ShapeDtypeStruct((leaf_nodes, columns), BF16),
        [pltpu.VMEM((interface, columns), F32), pltpu.VMEM((leaf_nodes, columns), F32)],
        1,
        (2 * leaf_nodes * leaf_nodes * columns, 2 * leaf_nodes * leaf_nodes),
        pos,
        final_own,
        final_other,
        local_map,
        local_load,
    )
    return result[None, None]


SPLITS = {(16, 32): (8, 2, 4, 8)}


def solution(mesh):
    shape = SPLITS.get(tuple(mesh.devices.shape), (2, 2, 2, 2))
    split = Mesh(mesh.devices.reshape(shape), ("z", "c", "x", "y"))
    grp, dom = ("z", "c"), ("x", "y")
    return jax.shard_map(
        on_device,
        mesh=split,
        in_specs=(
            P(dom, grp, None, None),
            P(dom, grp, None, None),
            P(dom, grp, None),
            P(dom, grp, None),
            P(dom, None, None),
            P(dom, None, None),
        ),
        out_specs=P(dom, grp, None, None),
        check_vma=False,
    )
```

```python
import functools

import jax
import jax.numpy as jnp
from jax import lax
from jax.experimental import pallas as pl
from jax.experimental.pallas import tpu as pltpu
from jax.sharding import Mesh
from jax.sharding import PartitionSpec as P


F32 = jnp.float32
BF16 = jnp.bfloat16
GRP = ("z", "c")
NT = (((1,), (1,)), ((), ()))
VM = pl.BlockSpec(memory_space=pltpu.VMEM)
SM = pl.BlockSpec(memory_space=pltpu.SMEM)
MIB = 1024 * 1024


def call(kernel, outs, scratch, smem, cost, *args, grant=16):
    specs = [SM] * smem + [VM] * (len(args) - smem)
    flops, moved = cost
    return pl.pallas_call(
        kernel,
        out_shape=outs,
        in_specs=specs,
        out_specs=jax.tree.map(lambda _: VM, outs),
        scratch_shapes=scratch,
        compiler_params=pltpu.CompilerParams(vmem_limit_bytes=grant * MIB),
        cost_estimate=pl.CostEstimate(flops=flops, bytes_accessed=moved, transcendentals=0),
    )(*args)


def exchange(value, axis):
    return lax.all_to_all(value, axis, 0, 0)


def spread_rows(pos, map_ref, load_ref, keep_ref, send_ref, contrib, rows):
    contrib[...] = (
        jnp.dot(map_ref[...], load_ref[...], preferred_element_type=F32).astype(BF16).astype(F32)
    )
    rows[...] = jnp.zeros_like(rows)
    count = contrib.shape[0]
    unroll = 16

    def some(turn, carry):
        base = pl.multiple_of(turn * unroll, unroll)
        for k in range(unroll):
            rows[pl.ds(pos[base + k], 1), :] = contrib[pl.ds(base + k, 1), :]
        return carry

    lax.fori_loop(0, count // unroll, some, 0)
    half = keep_ref.shape[0]
    keep_ref[...] = rows[:half].astype(BF16)
    send_ref[...] = rows[half:].astype(BF16)


def first_pieces(map_ref, west_ref, east_ref, out_ref, rows, turned, *, stride):
    count = map_ref.shape[0] // stride
    for k in range(count):
        pair = map_ref[k * stride : (k + 1) * stride, :].astype(F32)
        rows[k : k + 1, :] = pair[0:1]
        rows[count + k : count + k + 1, :] = pair[1:2]
    turned[...] = rows[...].T
    n = west_ref.shape[0]

    def coupled(at, coupling):
        picked = turned[pl.ds(at, n, stride=stride), :].T.astype(BF16)
        high, low = halves(coupling)
        return jnp.dot(picked, high, preferred_element_type=F32) + jnp.dot(
            picked, low, preferred_element_type=F32
        )

    by_west = coupled(0, west_ref[...]).astype(BF16)
    by_east = coupled(1, east_ref[...]).astype(BF16)
    slim = out_ref.shape[2]
    sides = n // slim
    for g in range(out_ref.shape[0]):
        side = slice(g % sides * slim, (g % sides + 1) * slim)
        out_ref[g, 0:count] = by_west[count:, side]
        out_ref[g, count : 2 * count] = by_west[:count, side]
        out_ref[g, 2 * count : 3 * count] = by_east[:count, side]
        for k in range(sides):
            block = slice((g * sides + k) * slim, (g * sides + k + 1) * slim)
            at = 3 * count + k * count
            out_ref[g, at : at + count] = rows[count:, block].astype(BF16)
            at = at + sides * count
            out_ref[g, at : at + count] = rows[:count, block].astype(BF16)


def couple_rows(map_ref, west_ref, east_ref, out_ref, turned, *, stride):
    parts, interface, slim = turned.shape
    n = west_ref.shape[0]
    for p in range(parts):
        block = slice(p * slim, (p + 1) * slim)
        for at in range(0, interface, n):
            turned[p, at : at + n] = map_ref[block, at : at + n].astype(F32).T
        for side, coupling in enumerate((west_ref, east_ref)):
            picked = turned[p, pl.ds(side, n, stride=stride), :].T.astype(BF16)
            high, low = halves(coupling[...])
            out_ref[block, side * n : (side + 1) * n] = (
                jnp.dot(picked, high, preferred_element_type=F32)
                + jnp.dot(picked, low, preferred_element_type=F32)
            ).astype(BF16)


def lay_halves(target, slot, side, mine, other):
    rows = mine.shape[0]
    target[slot, pl.ds(pl.multiple_of(side * rows, rows), rows), :] = mine
    target[slot, pl.ds(pl.multiple_of((1 - side) * rows, rows), rows), :] = other


def sort_maps(got_ref, maps_ref):
    peers = got_ref.shape[0]
    n = maps_ref.shape[0] // 3
    nodes = n // peers
    for g in range(peers):
        for k in range(3):
            maps_ref[k * n + g * nodes : k * n + (g + 1) * nodes] = got_ref[
                g, k * nodes : (k + 1) * nodes
            ]


def face_parts(parts_ref, rows_ref, loads_ref, out_ref, order):
    total = parts_ref[0].astype(F32)
    for z in range(1, parts_ref.shape[0]):
        total = total + parts_ref[z].astype(F32)
    loads = total.astype(BF16)
    loads_ref[...] = loads
    peers, high, slim = rows_ref.shape
    sides = order.shape[1] // slim
    nodes = high // (3 + 2 * sides)
    for g in range(peers):
        for k in range(sides):
            block = slice(k * slim, (k + 1) * slim)
            at = (3 + k) * nodes
            order[g * nodes : (g + 1) * nodes, block] = rows_ref[g, at : at + nodes]
            at = at + sides * nodes
            order[(peers + g) * nodes : (peers + g + 1) * nodes, block] = rows_ref[
                g, at : at + nodes
            ]
    lines = lax.dot_general(total.T.astype(BF16), order[...], NT, preferred_element_type=F32)
    part = out_ref.shape[1]
    for g in range(peers):
        out_ref[g] = lines[g * part : (g + 1) * part].astype(BF16)


def face_sum(got_ref, out_ref):
    total = got_ref[0].astype(F32)
    for g in range(1, got_ref.shape[0]):
        total = total + got_ref[g].astype(F32)
    line = total.astype(BF16)
    for y in range(out_ref.shape[0]):
        out_ref[y] = line


def halves(value):
    high = value.astype(BF16)
    low = (value - high.astype(F32)).astype(BF16)
    return high, low


def exact_right(left, value):
    high, low = halves(value)
    return jnp.dot(left, high, preferred_element_type=F32) + jnp.dot(
        left, low, preferred_element_type=F32
    )


def exact_rows(value, right):
    rows = value.shape[0]
    high, low = halves(value)
    both = lax.dot_general(
        jnp.concatenate([high, low], axis=0), right, NT, preferred_element_type=F32
    )
    return both[:rows] + both[rows:]


def run_block(place, faces_ref, mine_ref, other_ref, ends_ref, own_maps_ref, own_ref, *scratch):
    state, right, through, given, sources, joined, maps_ref = scratch
    count, part, _ = faces_ref.shape
    slim = mine_ref.shape[2]
    n = maps_ref.shape[2]
    here, side = place[0], place[1]
    maps_ref[:, :, pl.ds(pl.multiple_of(side * slim, slim), slim)] = mine_ref[...]
    maps_ref[:, :, pl.ds(pl.multiple_of((1 - side) * slim, slim), slim)] = other_ref[...]
    unit = (
        lax.broadcasted_iota(jnp.int32, (n, n), 0) == lax.broadcasted_iota(jnp.int32, (n, n), 1)
    ).astype(F32)
    state[...] = unit
    right[:, 0:n] = unit
    right[:, n : 2 * n] = jnp.zeros((n, n), F32)
    given[...] = jnp.zeros_like(given)

    def onward(j, carry):
        value = state[...]
        east = given[:, 0:n]

        @pl.when(j == here)
        def _():
            own_maps_ref[0:n] = value.astype(BF16)
            own_ref[:, 0:n] = east

        maps = maps_ref[j, 0 : 2 * n, :]
        both = exact_right(maps, value)
        moved = faces_ref[j].astype(F32) + exact_rows(east, maps)
        state[...] = both[:n]
        through[j] = both[n:]
        given[:, 0:n] = moved[:, 0:n]
        sources[j] = moved[:, n : 2 * n]
        return carry

    lax.fori_loop(0, count, onward, 0)

    def back(turn, carry):
        j = count - 1 - turn
        value = right[...]
        west = given[:, n : 2 * n]

        @pl.when(j == here)
        def _():
            own_maps_ref[n : 2 * n] = value[:, 0:n].astype(BF16)
            own_maps_ref[2 * n : 3 * n] = value[:, n : 2 * n].astype(BF16)
            own_ref[:, n : 2 * n] = west

        maps = maps_ref[j, 2 * n : 3 * n, :]
        both = exact_right(maps, value)
        moved = sources[j] + exact_rows(west, maps)
        right[:, 0:n] = both[:, 0:n]
        right[:, n : 2 * n] = both[:, n : 2 * n] + through[j]
        given[:, n : 2 * n] = moved
        return carry

    lax.fori_loop(0, count, back, 0)
    ends = jnp.concatenate([given[:, 0:n], given[:, n : 2 * n]], axis=0).astype(BF16)
    joined[0:n] = state[...].astype(BF16)
    joined[n : 2 * n] = right[:, 0:n].astype(BF16)
    joined[2 * n : 3 * n] = right[:, n : 2 * n].astype(BF16)
    rows = ends_ref.shape[1] - 2 * part
    half = joined[pl.ds(pl.multiple_of(side * rows, rows), rows), :]
    for x in range(ends_ref.shape[0]):
        ends_ref[x, 0:rows] = half
        ends_ref[x, rows : rows + 2 * part] = ends


def meet_values(place, ends_ref, other_ref, maps_ref, own_ref, out_ref, entering, joined_ref):
    count, _, n = ends_ref.shape
    part = own_ref.shape[0]
    here, side = place[0], place[1]
    rows = ends_ref.shape[1] - 2 * part
    for b in range(count):
        lay_halves(joined_ref, b, side, ends_ref[b, 0:rows], other_ref[b, 0:rows])
    east = jnp.zeros((part, n), F32)
    sources = []
    for b in range(count):

        @pl.when(here == b)
        def _(east=east):
            entering[:, 0:n] = east

        end = ends_ref[b, rows : rows + 2 * part].astype(F32)
        source = end[part : 2 * part]
        if b:
            source = source + exact_rows(east, joined_ref[b, 2 * n : 3 * n, :])
        sources.append(source)
        east = end[0:part] + (exact_rows(east, joined_ref[b, 0:n, :]) if b else 0.0)
    west = jnp.zeros((part, n), F32)
    for b in range(count - 1, -1, -1):

        @pl.when(here == b)
        def _(west=west):
            entering[:, n : 2 * n] = west

        west = sources[b] + (
            exact_rows(west, joined_ref[b, n : 2 * n, :]) if b < count - 1 else 0.0
        )
    east = entering[:, 0:n]
    west = entering[:, n : 2 * n]
    own = own_ref[...]
    met_east = own[:, 0:n] + exact_rows(east, maps_ref[0:n])
    met_west = (
        own[:, n : 2 * n]
        + exact_rows(west, maps_ref[n : 2 * n])
        + exact_rows(east, maps_ref[2 * n : 3 * n])
    )
    met = jnp.concatenate([met_east, met_west], axis=1).astype(BF16)
    for g in range(out_ref.shape[0]):
        out_ref[g] = met


def leaf_result(pos, own_ref, other_ref, map_ref, load_ref, out_ref, rows, picked):
    half = own_ref.shape[0]
    rows[0:half] = own_ref[...].astype(F32)
    rows[half : 2 * half] = other_ref[...].astype(F32)
    count = picked.shape[0]
    unroll = 16

    def some(turn, carry):
        base = pl.multiple_of(turn * unroll, unroll)
        for k in range(unroll):
            picked[pl.ds(base + k, 1), :] = rows[pl.ds(pos[base + k], 1), :]
        return carry

    lax.fori_loop(0, count // unroll, some, 0)
    turned = picked[...].T.astype(BF16)
    result = jnp.dot(turned, map_ref[...], preferred_element_type=F32)
    out_ref[...] = (result.T + load_ref[...].astype(F32)).astype(BF16)


def on_device(leaf_load, leaf_map, group_map, node_index, west_coupling, east_coupling):
    local_map, local_load, nodes_of = leaf_map[0, 0], leaf_load[0, 0], node_index[0, 0]
    rows_map, west, east = group_map[0], west_coupling[0], east_coupling[0]
    nz, nc = lax.axis_size("z"), lax.axis_size("c")
    nx, ny = lax.axis_size("x"), lax.axis_size("y")
    peers = nz * nc
    leaf_nodes, columns = local_load.shape
    width, interface = rows_map.shape
    n = west.shape[0]
    stride = interface // n
    nodes = n // peers
    part = columns // peers
    half = interface // nc
    side = lax.axis_index("c")
    core = side.astype(jnp.int32)
    at_y = jnp.stack([lax.axis_index("y").astype(jnp.int32), core])
    at_x = jnp.stack([lax.axis_index("x").astype(jnp.int32), core])
    swap = [(0, 1), (1, 0)]

    pieces = call(
        functools.partial(first_pieces, stride=stride),
        jax.ShapeDtypeStruct((peers, (3 + 2 * nc) * nodes, width // nc), BF16),
        [pltpu.VMEM((2 * nodes, interface), F32), pltpu.VMEM((interface, 2 * nodes), F32)],
        0,
        (8 * nodes * n * n, 2 * width * interface),
        rows_map,
        west,
        east,
        grant=52,
    )
    pieces = exchange(pieces, GRP)

    owner = nodes_of // width
    pos = ((owner % nc) ^ side) * half + (owner // nc) * width + nodes_of % width
    keep, send = call(
        spread_rows,
        (jax.ShapeDtypeStruct((half, columns), BF16),) * 2,
        [pltpu.VMEM((leaf_nodes, columns), F32), pltpu.VMEM((interface, columns), F32)],
        1,
        (2 * leaf_nodes * leaf_nodes * columns, 6 * leaf_nodes * leaf_nodes),
        pos,
        local_map,
        local_load,
    )
    got = lax.ppermute(send, "c", swap)
    paired = (keep.astype(F32) + got.astype(F32)).astype(BF16)
    pieces, paired = lax.optimization_barrier((pieces, paired))
    maps = call(
        sort_maps,
        jax.ShapeDtypeStruct((3 * n, n // nc), BF16),
        [],
        0,
        (1000, 8 * n * n),
        pieces,
    )
    run_half = lax.all_gather(maps, "y")

    parts = exchange(paired.reshape(nz, width, columns), "z")
    late_map, _ = lax.optimization_barrier((rows_map, maps))
    coupled = call(
        functools.partial(couple_rows, stride=stride),
        jax.ShapeDtypeStruct((width, 2 * n), BF16),
        [pltpu.VMEM((width // 128, interface, 128), F32)],
        0,
        (8 * width * n * n, 4 * width * interface),
        late_map,
        west,
        east,
    )

    loads, faces = call(
        face_parts,
        (
            jax.ShapeDtypeStruct((width, columns), BF16),
            jax.ShapeDtypeStruct((peers, part, 2 * n), BF16),
        ),
        [pltpu.VMEM((2 * n, width), BF16)],
        0,
        (4 * n * width * columns, 4 * n * width),
        parts,
        pieces,
    )
    faces = lax.all_to_all(faces, GRP, 0, 0)
    line = call(
        face_sum,
        jax.ShapeDtypeStruct((ny, part, 2 * n), BF16),
        [],
        0,
        (1000, 4 * n * columns),
        faces,
    )

    all_loads = lax.all_gather(loads, GRP, axis=0, tiled=True)

    run_half, line = lax.optimization_barrier((run_half, line))
    run_other = lax.ppermute(run_half, "c", swap)
    line = exchange(line, "y")
    ends, own_maps, own_values = call(
        run_block,
        (
            jax.ShapeDtypeStruct((nx, 3 * n // nc + 2 * part, n), BF16),
            jax.ShapeDtypeStruct((3 * n, n), BF16),
            jax.ShapeDtypeStruct((part, 2 * n), F32),
        ),
        [
            pltpu.VMEM((n, n), F32),
            pltpu.VMEM((n, 2 * n), F32),
            pltpu.VMEM((ny, n, n), F32),
            pltpu.VMEM((part, 2 * n), F32),
            pltpu.VMEM((ny, part, n), F32),
            pltpu.VMEM((3 * n, n), BF16),
            pltpu.VMEM((ny, 3 * n, n), BF16),
        ],
        1,
        (16 * ny * n**3, 6 * ny * n * n),
        at_y,
        line,
        run_half,
        run_other,
    )
    ends = lax.all_to_all(ends, "x", 0, 0)
    other_ends = lax.ppermute(ends, "c", swap)
    met = call(
        meet_values,
        jax.ShapeDtypeStruct((peers, part, 2 * n), BF16),
        [pltpu.VMEM((part, 2 * n), F32), pltpu.VMEM((nx, 3 * n, n), BF16)],
        1,
        (12 * nx * n * n * 16, 6 * nx * n * n),
        at_x,
        ends,
        other_ends,
        own_maps,
        own_values,
    )
    met_blocks = lax.all_to_all(met, GRP, 0, 0)

    all_loads, _ = lax.optimization_barrier((all_loads, met))
    initial = jnp.dot(rows_map, all_loads, preferred_element_type=F32)
    met = met_blocks.reshape(columns, 2 * n)
    final = initial + lax.dot_general(coupled, met, NT, preferred_element_type=F32)
    final = jnp.broadcast_to(final.astype(BF16), (nz, width, columns))
    final_own = lax.all_to_all(final, "z", 0, 0).reshape(half, columns)
    final_other = lax.ppermute(final_own, "c", swap)
    result = call(
        leaf_result,
        jax.ShapeDtypeStruct((leaf_nodes, columns), BF16),
        [pltpu.VMEM((interface, columns), F32), pltpu.VMEM((leaf_nodes, columns), F32)],
        1,
        (2 * leaf_nodes * leaf_nodes * columns, 2 * leaf_nodes * leaf_nodes),
        pos,
        final_own,
        final_other,
        local_map,
        local_load,
    )
    return result[None, None]


SPLITS = {(16, 32): (8, 2, 4, 8)}


def solution(mesh):
    shape = SPLITS.get(tuple(mesh.devices.shape), (2, 2, 2, 2))
    split = Mesh(mesh.devices.reshape(shape), ("z", "c", "x", "y"))
    grp, dom = ("z", "c"), ("x", "y")
    return jax.shard_map(
        on_device,
        mesh=split,
        in_specs=(
            P(dom, grp, None, None),
            P(dom, grp, None, None),
            P(dom, grp, None),
            P(dom, grp, None),
            P(dom, None, None),
            P(dom, None, None),
        ),
        out_specs=P(dom, grp, None, None),
        check_vma=False,
    )
```

```python
import functools

import jax
import jax.numpy as jnp
from jax import lax
from jax.experimental import pallas as pl
from jax.experimental.pallas import tpu as pltpu
from jax.sharding import Mesh
from jax.sharding import PartitionSpec as P


F32 = jnp.float32
BF16 = jnp.bfloat16
GRP = ("z", "c")
NT = (((1,), (1,)), ((), ()))
VM = pl.BlockSpec(memory_space=pltpu.VMEM)
SM = pl.BlockSpec(memory_space=pltpu.SMEM)
MIB = 1024 * 1024


def call(kernel, outs, scratch, smem, cost, *args, grant=16):
    specs = [SM] * smem + [VM] * (len(args) - smem)
    flops, moved = cost
    return pl.pallas_call(
        kernel,
        out_shape=outs,
        in_specs=specs,
        out_specs=jax.tree.map(lambda _: VM, outs),
        scratch_shapes=scratch,
        compiler_params=pltpu.CompilerParams(vmem_limit_bytes=grant * MIB),
        cost_estimate=pl.CostEstimate(flops=flops, bytes_accessed=moved, transcendentals=0),
    )(*args)


def exchange(value, axis):
    return lax.all_to_all(value, axis, 0, 0)


def spread_rows(pos, map_ref, load_ref, keep_ref, send_ref, contrib, rows):
    contrib[...] = (
        jnp.dot(map_ref[...], load_ref[...], preferred_element_type=F32).astype(BF16).astype(F32)
    )
    rows[...] = jnp.zeros_like(rows)
    count = contrib.shape[0]
    unroll = 16

    def some(turn, carry):
        base = pl.multiple_of(turn * unroll, unroll)
        for k in range(unroll):
            rows[pl.ds(pos[base + k], 1), :] = contrib[pl.ds(base + k, 1), :]
        return carry

    lax.fori_loop(0, count // unroll, some, 0)
    half = keep_ref.shape[0]
    keep_ref[...] = rows[:half].astype(BF16)
    send_ref[...] = rows[half:].astype(BF16)


def first_pieces(map_ref, west_ref, east_ref, out_ref, rows, turned, *, stride):
    count = map_ref.shape[0] // stride
    for k in range(count):
        pair = map_ref[k * stride : (k + 1) * stride, :].astype(F32)
        rows[k : k + 1, :] = pair[0:1]
        rows[count + k : count + k + 1, :] = pair[1:2]
    turned[...] = rows[...].T
    n = west_ref.shape[0]

    def coupled(at, coupling):
        picked = turned[pl.ds(at, n, stride=stride), :].T.astype(BF16)
        high, low = halves(coupling)
        return jnp.dot(picked, high, preferred_element_type=F32) + jnp.dot(
            picked, low, preferred_element_type=F32
        )

    by_west = coupled(0, west_ref[...]).astype(BF16)
    by_east = coupled(1, east_ref[...]).astype(BF16)
    slim = out_ref.shape[2]
    sides = n // slim
    for g in range(out_ref.shape[0]):
        side = slice(g % sides * slim, (g % sides + 1) * slim)
        out_ref[g, 0:count] = by_west[count:, side]
        out_ref[g, count : 2 * count] = by_west[:count, side]
        out_ref[g, 2 * count : 3 * count] = by_east[:count, side]
        for k in range(sides):
            block = slice((g * sides + k) * slim, (g * sides + k + 1) * slim)
            at = 3 * count + k * count
            out_ref[g, at : at + count] = rows[count:, block].astype(BF16)
            at = at + sides * count
            out_ref[g, at : at + count] = rows[:count, block].astype(BF16)


def couple_rows(map_ref, west_ref, east_ref, out_ref, turned, *, stride):
    parts, interface, slim = turned.shape
    n = west_ref.shape[0]
    for p in range(parts):
        block = slice(p * slim, (p + 1) * slim)
        for at in range(0, interface, n):
            turned[p, at : at + n] = map_ref[block, at : at + n].astype(F32).T
        for side, coupling in enumerate((west_ref, east_ref)):
            picked = turned[p, pl.ds(side, n, stride=stride), :].T.astype(BF16)
            high, low = halves(coupling[...])
            out_ref[block, side * n : (side + 1) * n] = (
                jnp.dot(picked, high, preferred_element_type=F32)
                + jnp.dot(picked, low, preferred_element_type=F32)
            ).astype(BF16)


def lay_halves(target, slot, side, mine, other):
    rows = mine.shape[0]
    target[slot, pl.ds(pl.multiple_of(side * rows, rows), rows), :] = mine
    target[slot, pl.ds(pl.multiple_of((1 - side) * rows, rows), rows), :] = other


def sort_maps(got_ref, maps_ref):
    peers = got_ref.shape[0]
    n = maps_ref.shape[0] // 3
    nodes = n // peers
    for g in range(peers):
        for k in range(3):
            maps_ref[k * n + g * nodes : k * n + (g + 1) * nodes] = got_ref[
                g, k * nodes : (k + 1) * nodes
            ]


def face_parts(parts_ref, rows_ref, loads_ref, out_ref, order):
    total = parts_ref[0].astype(F32)
    for z in range(1, parts_ref.shape[0]):
        total = total + parts_ref[z].astype(F32)
    loads = total.astype(BF16)
    loads_ref[...] = loads
    peers, high, slim = rows_ref.shape
    sides = order.shape[1] // slim
    nodes = high // (3 + 2 * sides)
    for g in range(peers):
        for k in range(sides):
            block = slice(k * slim, (k + 1) * slim)
            at = (3 + k) * nodes
            order[g * nodes : (g + 1) * nodes, block] = rows_ref[g, at : at + nodes]
            at = at + sides * nodes
            order[(peers + g) * nodes : (peers + g + 1) * nodes, block] = rows_ref[
                g, at : at + nodes
            ]
    lines = lax.dot_general(total.T.astype(BF16), order[...], NT, preferred_element_type=F32)
    part = out_ref.shape[1]
    for g in range(peers):
        out_ref[g] = lines[g * part : (g + 1) * part].astype(BF16)


def face_sum(got_ref, out_ref):
    total = got_ref[0].astype(F32)
    for g in range(1, got_ref.shape[0]):
        total = total + got_ref[g].astype(F32)
    line = total.astype(BF16)
    for y in range(out_ref.shape[0]):
        out_ref[y] = line


def halves(value):
    high = value.astype(BF16)
    low = (value - high.astype(F32)).astype(BF16)
    return high, low


def exact_right(left, value):
    high, low = halves(value)
    return jnp.dot(left, high, preferred_element_type=F32) + jnp.dot(
        left, low, preferred_element_type=F32
    )


def exact_rows(value, right):
    rows = value.shape[0]
    high, low = halves(value)
    both = lax.dot_general(
        jnp.concatenate([high, low], axis=0), right, NT, preferred_element_type=F32
    )
    return both[:rows] + both[rows:]


def run_block(place, faces_ref, mine_ref, other_ref, ends_ref, own_maps_ref, own_ref, *scratch):
    state, right, through, given, sources, joined = scratch
    count, part, _ = faces_ref.shape
    slim = mine_ref.shape[2]
    n = state.shape[0]
    here, side = place[0], place[1]

    def halves_at(start):
        first = pl.multiple_of(start + side * slim, slim)
        second = pl.multiple_of(start + (1 - side) * slim, slim)
        return pl.ds(first, slim), pl.ds(second, slim)

    def maps_at(j, rows):
        return jnp.concatenate([mine_ref[j, rows, :], other_ref[j, rows, :]], axis=1)

    def rows_met(ref):
        first, second = halves_at(0)
        return jnp.concatenate([ref[first, :], ref[second, :]], axis=0)

    def lanes_met(start):
        first, second = halves_at(start)
        return jnp.concatenate([given[:, first], given[:, second]], axis=1)

    unit = (
        lax.broadcasted_iota(jnp.int32, (n, n), 0) == lax.broadcasted_iota(jnp.int32, (n, n), 1)
    ).astype(F32)
    state[...] = unit
    right[:, 0:n] = unit
    right[:, n : 2 * n] = jnp.zeros((n, n), F32)
    given[...] = jnp.zeros_like(given)

    def onward(j, carry):
        @pl.when(j == here)
        def _():
            own_maps_ref[0:n] = state[...].astype(BF16)
            own_ref[:, 0:n] = given[:, 0:n]

        maps = maps_at(j, slice(0, 2 * n))
        both = exact_right(maps, rows_met(state))
        moved = faces_ref[j].astype(F32) + exact_rows(lanes_met(0), maps)
        state[...] = both[:n]
        through[j] = both[n:]
        given[:, 0:n] = moved[:, 0:n]
        sources[j] = moved[:, n : 2 * n]
        return carry

    lax.fori_loop(0, count, onward, 0)

    def back(turn, carry):
        j = count - 1 - turn

        @pl.when(j == here)
        def _():
            own_maps_ref[n : 2 * n] = right[:, 0:n].astype(BF16)
            own_maps_ref[2 * n : 3 * n] = right[:, n : 2 * n].astype(BF16)
            own_ref[:, n : 2 * n] = given[:, n : 2 * n]

        maps = maps_at(j, slice(2 * n, 3 * n))
        both = exact_right(maps, rows_met(right))
        moved = sources[j] + exact_rows(lanes_met(n), maps)
        right[:, 0:n] = both[:, 0:n]
        right[:, n : 2 * n] = both[:, n : 2 * n] + through[j]
        given[:, n : 2 * n] = moved
        return carry

    lax.fori_loop(0, count, back, 0)
    ends = jnp.concatenate([given[:, 0:n], given[:, n : 2 * n]], axis=0).astype(BF16)
    joined[0:n] = state[...].astype(BF16)
    joined[n : 2 * n] = right[:, 0:n].astype(BF16)
    joined[2 * n : 3 * n] = right[:, n : 2 * n].astype(BF16)
    rows = ends_ref.shape[1] - 2 * part
    half = joined[pl.ds(pl.multiple_of(side * rows, rows), rows), :]
    for x in range(ends_ref.shape[0]):
        ends_ref[x, 0:rows] = half
        ends_ref[x, rows : rows + 2 * part] = ends


def meet_values(place, ends_ref, other_ref, maps_ref, own_ref, out_ref, entering, joined_ref):
    count, _, n = ends_ref.shape
    part = own_ref.shape[0]
    here, side = place[0], place[1]
    rows = ends_ref.shape[1] - 2 * part
    for b in range(count):
        lay_halves(joined_ref, b, side, ends_ref[b, 0:rows], other_ref[b, 0:rows])
    east = jnp.zeros((part, n), F32)
    sources = []
    for b in range(count):

        @pl.when(here == b)
        def _(east=east):
            entering[:, 0:n] = east

        end = ends_ref[b, rows : rows + 2 * part].astype(F32)
        source = end[part : 2 * part]
        if b:
            source = source + exact_rows(east, joined_ref[b, 2 * n : 3 * n, :])
        sources.append(source)
        east = end[0:part] + (exact_rows(east, joined_ref[b, 0:n, :]) if b else 0.0)
    west = jnp.zeros((part, n), F32)
    for b in range(count - 1, -1, -1):

        @pl.when(here == b)
        def _(west=west):
            entering[:, n : 2 * n] = west

        west = sources[b] + (
            exact_rows(west, joined_ref[b, n : 2 * n, :]) if b < count - 1 else 0.0
        )
    east = entering[:, 0:n]
    west = entering[:, n : 2 * n]
    own = own_ref[...]
    met_east = own[:, 0:n] + exact_rows(east, maps_ref[0:n])
    met_west = (
        own[:, n : 2 * n]
        + exact_rows(west, maps_ref[n : 2 * n])
        + exact_rows(east, maps_ref[2 * n : 3 * n])
    )
    met = jnp.concatenate([met_east, met_west], axis=1).astype(BF16)
    for g in range(out_ref.shape[0]):
        out_ref[g] = met


def leaf_result(pos, own_ref, other_ref, map_ref, load_ref, out_ref, rows, picked):
    half = own_ref.shape[0]
    rows[0:half] = own_ref[...].astype(F32)
    rows[half : 2 * half] = other_ref[...].astype(F32)
    count = picked.shape[0]
    unroll = 16

    def some(turn, carry):
        base = pl.multiple_of(turn * unroll, unroll)
        for k in range(unroll):
            picked[pl.ds(base + k, 1), :] = rows[pl.ds(pos[base + k], 1), :]
        return carry

    lax.fori_loop(0, count // unroll, some, 0)
    turned = picked[...].T.astype(BF16)
    result = jnp.dot(turned, map_ref[...], preferred_element_type=F32)
    out_ref[...] = (result.T + load_ref[...].astype(F32)).astype(BF16)


def on_device(leaf_load, leaf_map, group_map, node_index, west_coupling, east_coupling):
    local_map, local_load, nodes_of = leaf_map[0, 0], leaf_load[0, 0], node_index[0, 0]
    rows_map, west, east = group_map[0], west_coupling[0], east_coupling[0]
    nz, nc = lax.axis_size("z"), lax.axis_size("c")
    nx, ny = lax.axis_size("x"), lax.axis_size("y")
    peers = nz * nc
    leaf_nodes, columns = local_load.shape
    width, interface = rows_map.shape
    n = west.shape[0]
    stride = interface // n
    nodes = n // peers
    part = columns // peers
    half = interface // nc
    side = lax.axis_index("c")
    core = side.astype(jnp.int32)
    at_y = jnp.stack([lax.axis_index("y").astype(jnp.int32), core])
    at_x = jnp.stack([lax.axis_index("x").astype(jnp.int32), core])
    swap = [(0, 1), (1, 0)]

    pieces = call(
        functools.partial(first_pieces, stride=stride),
        jax.ShapeDtypeStruct((peers, (3 + 2 * nc) * nodes, width // nc), BF16),
        [pltpu.VMEM((2 * nodes, interface), F32), pltpu.VMEM((interface, 2 * nodes), F32)],
        0,
        (8 * nodes * n * n, 2 * width * interface),
        rows_map,
        west,
        east,
        grant=52,
    )
    pieces = exchange(pieces, GRP)

    owner = nodes_of // width
    pos = ((owner % nc) ^ side) * half + (owner // nc) * width + nodes_of % width
    keep, send = call(
        spread_rows,
        (jax.ShapeDtypeStruct((half, columns), BF16),) * 2,
        [pltpu.VMEM((leaf_nodes, columns), F32), pltpu.VMEM((interface, columns), F32)],
        1,
        (2 * leaf_nodes * leaf_nodes * columns, 6 * leaf_nodes * leaf_nodes),
        pos,
        local_map,
        local_load,
    )
    got = lax.ppermute(send, "c", swap)
    paired = (keep.astype(F32) + got.astype(F32)).astype(BF16)
    pieces, paired = lax.optimization_barrier((pieces, paired))
    maps = call(
        sort_maps,
        jax.ShapeDtypeStruct((3 * n, n // nc), BF16),
        [],
        0,
        (1000, 8 * n * n),
        pieces,
    )
    run_half = lax.all_gather(maps, "y")

    parts = exchange(paired.reshape(nz, width, columns), "z")
    late_map, _ = lax.optimization_barrier((rows_map, maps))
    coupled = call(
        functools.partial(couple_rows, stride=stride),
        jax.ShapeDtypeStruct((width, 2 * n), BF16),
        [pltpu.VMEM((width // 128, interface, 128), F32)],
        0,
        (8 * width * n * n, 4 * width * interface),
        late_map,
        west,
        east,
    )

    loads, faces = call(
        face_parts,
        (
            jax.ShapeDtypeStruct((width, columns), BF16),
            jax.ShapeDtypeStruct((peers, part, 2 * n), BF16),
        ),
        [pltpu.VMEM((2 * n, width), BF16)],
        0,
        (4 * n * width * columns, 4 * n * width),
        parts,
        pieces,
    )
    faces = lax.all_to_all(faces, GRP, 0, 0)
    line = call(
        face_sum,
        jax.ShapeDtypeStruct((ny, part, 2 * n), BF16),
        [],
        0,
        (1000, 4 * n * columns),
        faces,
    )

    all_loads = lax.all_gather(loads, GRP, axis=0, tiled=True)

    run_other = lax.ppermute(run_half, "c", swap)
    line = exchange(line, "y")
    ends, own_maps, own_values = call(
        run_block,
        (
            jax.ShapeDtypeStruct((nx, 3 * n // nc + 2 * part, n), BF16),
            jax.ShapeDtypeStruct((3 * n, n), BF16),
            jax.ShapeDtypeStruct((part, 2 * n), F32),
        ),
        [
            pltpu.VMEM((n, n), F32),
            pltpu.VMEM((n, 2 * n), F32),
            pltpu.VMEM((ny, n, n), F32),
            pltpu.VMEM((part, 2 * n), F32),
            pltpu.VMEM((ny, part, n), F32),
            pltpu.VMEM((3 * n, n), BF16),
        ],
        1,
        (16 * ny * n**3, 6 * ny * n * n),
        at_y,
        line,
        run_half,
        run_other,
    )
    ends = lax.all_to_all(ends, "x", 0, 0)
    other_ends = lax.ppermute(ends, "c", swap)
    met = call(
        meet_values,
        jax.ShapeDtypeStruct((peers, part, 2 * n), BF16),
        [pltpu.VMEM((part, 2 * n), F32), pltpu.VMEM((nx, 3 * n, n), BF16)],
        1,
        (12 * nx * n * n * 16, 6 * nx * n * n),
        at_x,
        ends,
        other_ends,
        own_maps,
        own_values,
    )
    met_blocks = lax.all_to_all(met, GRP, 0, 0)

    all_loads, _ = lax.optimization_barrier((all_loads, met))
    initial = jnp.dot(rows_map, all_loads, preferred_element_type=F32)
    met = met_blocks.reshape(columns, 2 * n)
    final = initial + lax.dot_general(coupled, met, NT, preferred_element_type=F32)
    final = jnp.broadcast_to(final.astype(BF16), (nz, width, columns))
    final_own = lax.all_to_all(final, "z", 0, 0).reshape(half, columns)
    final_other = lax.ppermute(final_own, "c", swap)
    result = call(
        leaf_result,
        jax.ShapeDtypeStruct((leaf_nodes, columns), BF16),
        [pltpu.VMEM((interface, columns), F32), pltpu.VMEM((leaf_nodes, columns), F32)],
        1,
        (2 * leaf_nodes * leaf_nodes * columns, 2 * leaf_nodes * leaf_nodes),
        pos,
        final_own,
        final_other,
        local_map,
        local_load,
    )
    return result[None, None]


SPLITS = {(16, 32): (8, 2, 4, 8)}


def solution(mesh):
    shape = SPLITS.get(tuple(mesh.devices.shape), (2, 2, 2, 2))
    split = Mesh(mesh.devices.reshape(shape), ("z", "c", "x", "y"))
    grp, dom = ("z", "c"), ("x", "y")
    return jax.shard_map(
        on_device,
        mesh=split,
        in_specs=(
            P(dom, grp, None, None),
            P(dom, grp, None, None),
            P(dom, grp, None),
            P(dom, grp, None),
            P(dom, None, None),
            P(dom, None, None),
        ),
        out_specs=P(dom, grp, None, None),
        check_vma=False,
    )
```

```python
import functools

import jax
import jax.numpy as jnp
from jax import lax
from jax.experimental import pallas as pl
from jax.experimental.pallas import tpu as pltpu
from jax.sharding import Mesh
from jax.sharding import PartitionSpec as P


F32 = jnp.float32
BF16 = jnp.bfloat16
GRP = ("z", "c")
NT = (((1,), (1,)), ((), ()))
VM = pl.BlockSpec(memory_space=pltpu.VMEM)
SM = pl.BlockSpec(memory_space=pltpu.SMEM)
MIB = 1024 * 1024


def call(kernel, outs, scratch, smem, cost, *args, grant=16):
    specs = [SM] * smem + [VM] * (len(args) - smem)
    flops, moved = cost
    return pl.pallas_call(
        kernel,
        out_shape=outs,
        in_specs=specs,
        out_specs=jax.tree.map(lambda _: VM, outs),
        scratch_shapes=scratch,
        compiler_params=pltpu.CompilerParams(vmem_limit_bytes=int(grant * MIB)),
        cost_estimate=pl.CostEstimate(flops=flops, bytes_accessed=moved, transcendentals=0),
    )(*args)


def exchange(value, axis):
    return lax.all_to_all(value, axis, 0, 0)


def spread_rows(pos, map_ref, load_ref, keep_ref, send_ref, contrib, rows):
    contrib[...] = (
        jnp.dot(map_ref[...], load_ref[...], preferred_element_type=F32).astype(BF16).astype(F32)
    )
    rows[...] = jnp.zeros_like(rows)
    count = contrib.shape[0]
    unroll = 16

    def some(turn, carry):
        base = pl.multiple_of(turn * unroll, unroll)
        for k in range(unroll):
            rows[pl.ds(pos[base + k], 1), :] = contrib[pl.ds(base + k, 1), :]
        return carry

    lax.fori_loop(0, count // unroll, some, 0)
    half = keep_ref.shape[0]
    keep_ref[...] = rows[:half].astype(BF16)
    send_ref[...] = rows[half:].astype(BF16)


def first_pieces(map_ref, west_ref, east_ref, out_ref, rows, turned, *, stride):
    count = map_ref.shape[0] // stride
    for k in range(count):
        pair = map_ref[k * stride : (k + 1) * stride, :].astype(F32)
        rows[k : k + 1, :] = pair[0:1]
        rows[count + k : count + k + 1, :] = pair[1:2]
    turned[...] = rows[...].T
    n = west_ref.shape[0]

    def coupled(at, coupling):
        picked = turned[pl.ds(at, n, stride=stride), :].T.astype(BF16)
        high, low = halves(coupling)
        return jnp.dot(picked, high, preferred_element_type=F32) + jnp.dot(
            picked, low, preferred_element_type=F32
        )

    by_west = coupled(0, west_ref[...]).astype(BF16)
    by_east = coupled(1, east_ref[...]).astype(BF16)
    slim = out_ref.shape[2]
    sides = n // slim
    for g in range(out_ref.shape[0]):
        side = slice(g % sides * slim, (g % sides + 1) * slim)
        out_ref[g, 0:count] = by_west[count:, side]
        out_ref[g, count : 2 * count] = by_west[:count, side]
        out_ref[g, 2 * count : 3 * count] = by_east[:count, side]
        for k in range(sides):
            block = slice((g * sides + k) * slim, (g * sides + k + 1) * slim)
            at = 3 * count + k * count
            out_ref[g, at : at + count] = rows[count:, block].astype(BF16)
            at = at + sides * count
            out_ref[g, at : at + count] = rows[:count, block].astype(BF16)


def couple_rows(map_ref, west_ref, east_ref, out_ref, turned, *, stride):
    parts, interface, slim = turned.shape
    n = west_ref.shape[0]
    for p in range(parts):
        block = slice(p * slim, (p + 1) * slim)
        for at in range(0, interface, n):
            turned[p, at : at + n] = map_ref[block, at : at + n].astype(F32).T
        for side, coupling in enumerate((west_ref, east_ref)):
            picked = turned[p, pl.ds(side, n, stride=stride), :].T.astype(BF16)
            high, low = halves(coupling[...])
            out_ref[block, side * n : (side + 1) * n] = (
                jnp.dot(picked, high, preferred_element_type=F32)
                + jnp.dot(picked, low, preferred_element_type=F32)
            ).astype(BF16)


def sort_maps(got_ref, maps_ref):
    peers = got_ref.shape[0]
    n = maps_ref.shape[0] // 3
    nodes = n // peers
    for g in range(peers):
        for k in range(3):
            maps_ref[k * n + g * nodes : k * n + (g + 1) * nodes] = got_ref[
                g, k * nodes : (k + 1) * nodes
            ]


def face_parts(parts_ref, rows_ref, loads_ref, out_ref, order):
    total = parts_ref[0].astype(F32)
    for z in range(1, parts_ref.shape[0]):
        total = total + parts_ref[z].astype(F32)
    loads = total.astype(BF16)
    loads_ref[...] = loads
    peers, high, slim = rows_ref.shape
    sides = order.shape[1] // slim
    nodes = high // (3 + 2 * sides)
    for g in range(peers):
        for k in range(sides):
            block = slice(k * slim, (k + 1) * slim)
            at = (3 + k) * nodes
            order[g * nodes : (g + 1) * nodes, block] = rows_ref[g, at : at + nodes]
            at = at + sides * nodes
            order[(peers + g) * nodes : (peers + g + 1) * nodes, block] = rows_ref[
                g, at : at + nodes
            ]
    lines = lax.dot_general(total.T.astype(BF16), order[...], NT, preferred_element_type=F32)
    part = out_ref.shape[1]
    for g in range(peers):
        out_ref[g] = lines[g * part : (g + 1) * part].astype(BF16)


def face_sum(got_ref, out_ref):
    total = got_ref[0].astype(F32)
    for g in range(1, got_ref.shape[0]):
        total = total + got_ref[g].astype(F32)
    line = total.astype(BF16)
    for y in range(out_ref.shape[0]):
        out_ref[y] = line


def halves(value):
    high = value.astype(BF16)
    low = (value - high.astype(F32)).astype(BF16)
    return high, low


def exact_right(left, value):
    high, low = halves(value)
    return jnp.dot(left, high, preferred_element_type=F32) + jnp.dot(
        left, low, preferred_element_type=F32
    )


def exact_rows(value, right):
    rows = value.shape[0]
    high, low = halves(value)
    both = lax.dot_general(
        jnp.concatenate([high, low], axis=0), right, NT, preferred_element_type=F32
    )
    return both[:rows] + both[rows:]


def run_block(place, faces_ref, mine_ref, other_ref, ends_ref, own_maps_ref, own_ref, *scratch):
    state, right, through, given, sources, joined = scratch
    count, part, _ = faces_ref.shape
    slim = mine_ref.shape[2]
    n = state.shape[0]
    here, side = place[0], place[1]

    def halves_at(start):
        first = pl.multiple_of(start + side * slim, slim)
        second = pl.multiple_of(start + (1 - side) * slim, slim)
        return pl.ds(first, slim), pl.ds(second, slim)

    def maps_at(j, rows):
        return jnp.concatenate([mine_ref[j, rows, :], other_ref[j, rows, :]], axis=1)

    def rows_met(ref):
        first, second = halves_at(0)
        return jnp.concatenate([ref[first, :], ref[second, :]], axis=0)

    def lanes_met(start):
        first, second = halves_at(start)
        return jnp.concatenate([given[:, first], given[:, second]], axis=1)

    unit = (
        lax.broadcasted_iota(jnp.int32, (n, n), 0) == lax.broadcasted_iota(jnp.int32, (n, n), 1)
    ).astype(F32)
    state[...] = unit
    right[:, 0:n] = unit
    right[:, n : 2 * n] = jnp.zeros((n, n), F32)
    given[...] = jnp.zeros_like(given)

    def onward(j, carry):
        @pl.when(j == here)
        def _():
            own_maps_ref[0:n] = state[...].astype(BF16)
            own_ref[:, 0:n] = given[:, 0:n]

        maps = maps_at(j, slice(0, 2 * n))
        both = exact_right(maps, rows_met(state))
        moved = faces_ref[j].astype(F32) + exact_rows(lanes_met(0), maps)
        state[...] = both[:n]
        through[j] = both[n:]
        given[:, 0:n] = moved[:, 0:n]
        sources[j] = moved[:, n : 2 * n]
        return carry

    lax.fori_loop(0, count, onward, 0)

    def back(turn, carry):
        j = count - 1 - turn

        @pl.when(j == here)
        def _():
            own_maps_ref[n : 2 * n] = right[:, 0:n].astype(BF16)
            own_maps_ref[2 * n : 3 * n] = right[:, n : 2 * n].astype(BF16)
            own_ref[:, n : 2 * n] = given[:, n : 2 * n]

        maps = maps_at(j, slice(2 * n, 3 * n))
        both = exact_right(maps, rows_met(right))
        moved = sources[j] + exact_rows(lanes_met(n), maps)
        right[:, 0:n] = both[:, 0:n]
        right[:, n : 2 * n] = both[:, n : 2 * n] + through[j]
        given[:, n : 2 * n] = moved
        return carry

    lax.fori_loop(0, count, back, 0)
    ends = jnp.concatenate([given[:, 0:n], given[:, n : 2 * n]], axis=0).astype(BF16)
    joined[0:n] = state[...].astype(BF16)
    joined[n : 2 * n] = right[:, 0:n].astype(BF16)
    joined[2 * n : 3 * n] = right[:, n : 2 * n].astype(BF16)
    half = joined[:, pl.ds(pl.multiple_of(side * slim, slim), slim)]
    for x in range(ends_ref.shape[0]):
        ends_ref[x, 0 : 3 * n] = half
        for k in range(n // slim):
            at = 3 * n + 2 * part * k
            ends_ref[x, at : at + 2 * part] = ends[:, k * slim : (k + 1) * slim]


def meet_values(place, ends_ref, other_ref, maps_ref, own_ref, out_ref, entering):
    count, _, slim = ends_ref.shape
    n = maps_ref.shape[1]
    part = own_ref.shape[0]
    here, side = place[0], place[1]

    def through(value, b, rows):
        turned = jnp.concatenate([value[:, slim:], value[:, :slim]], axis=1)
        maps = jnp.concatenate([ends_ref[b, rows, :], other_ref[b, rows, :]], axis=1)
        return exact_rows(jnp.where(side == 0, value, turned), maps)

    def end_of(b):
        both = ends_ref[b, 3 * n : 3 * n + 2 * part * (n // slim)].astype(F32)
        pieces = [both[k * 2 * part : (k + 1) * 2 * part] for k in range(n // slim)]
        return jnp.concatenate(pieces, axis=1)

    east = jnp.zeros((part, n), F32)
    sources = []
    for b in range(count):

        @pl.when(here == b)
        def _(east=east):
            entering[:, 0:n] = east

        end = end_of(b)
        source = end[part : 2 * part]
        if b:
            source = source + through(east, b, slice(2 * n, 3 * n))
        sources.append(source)
        east = end[0:part] + (through(east, b, slice(0, n)) if b else 0.0)
    west = jnp.zeros((part, n), F32)
    for b in range(count - 1, -1, -1):

        @pl.when(here == b)
        def _(west=west):
            entering[:, n : 2 * n] = west

        west = sources[b] + (through(west, b, slice(n, 2 * n)) if b < count - 1 else 0.0)
    east = entering[:, 0:n]
    west = entering[:, n : 2 * n]
    own = own_ref[...]
    met_east = own[:, 0:n] + exact_rows(east, maps_ref[0:n])
    met_west = (
        own[:, n : 2 * n]
        + exact_rows(west, maps_ref[n : 2 * n])
        + exact_rows(east, maps_ref[2 * n : 3 * n])
    )
    met = jnp.concatenate([met_east, met_west], axis=1).astype(BF16)
    for g in range(out_ref.shape[0]):
        out_ref[g] = met


def leaf_result(pos, own_ref, other_ref, map_ref, load_ref, out_ref, rows, picked):
    half = own_ref.shape[0]
    rows[0:half] = own_ref[...].astype(F32)
    rows[half : 2 * half] = other_ref[...].astype(F32)
    count = picked.shape[0]
    unroll = 16

    def some(turn, carry):
        base = pl.multiple_of(turn * unroll, unroll)
        for k in range(unroll):
            picked[pl.ds(base + k, 1), :] = rows[pl.ds(pos[base + k], 1), :]
        return carry

    lax.fori_loop(0, count // unroll, some, 0)
    turned = picked[...].T.astype(BF16)
    result = jnp.dot(turned, map_ref[...], preferred_element_type=F32)
    out_ref[...] = (result.T + load_ref[...].astype(F32)).astype(BF16)


def on_device(leaf_load, leaf_map, group_map, node_index, west_coupling, east_coupling):
    local_map, local_load, nodes_of = leaf_map[0, 0], leaf_load[0, 0], node_index[0, 0]
    rows_map, west, east = group_map[0], west_coupling[0], east_coupling[0]
    nz, nc = lax.axis_size("z"), lax.axis_size("c")
    nx, ny = lax.axis_size("x"), lax.axis_size("y")
    peers = nz * nc
    leaf_nodes, columns = local_load.shape
    width, interface = rows_map.shape
    n = west.shape[0]
    stride = interface // n
    nodes = n // peers
    part = columns // peers
    half = interface // nc
    side = lax.axis_index("c")
    core = side.astype(jnp.int32)
    at_y = jnp.stack([lax.axis_index("y").astype(jnp.int32), core])
    at_x = jnp.stack([lax.axis_index("x").astype(jnp.int32), core])
    swap = [(0, 1), (1, 0)]

    pieces = call(
        functools.partial(first_pieces, stride=stride),
        jax.ShapeDtypeStruct((peers, (3 + 2 * nc) * nodes, width // nc), BF16),
        [pltpu.VMEM((2 * nodes, interface), F32), pltpu.VMEM((interface, 2 * nodes), F32)],
        0,
        (8 * nodes * n * n, 2 * width * interface),
        rows_map,
        west,
        east,
        grant=60.9,
    )
    pieces = exchange(pieces, GRP)

    owner = nodes_of // width
    pos = ((owner % nc) ^ side) * half + (owner // nc) * width + nodes_of % width
    keep, send = call(
        spread_rows,
        (jax.ShapeDtypeStruct((half, columns), BF16),) * 2,
        [pltpu.VMEM((leaf_nodes, columns), F32), pltpu.VMEM((interface, columns), F32)],
        1,
        (2 * leaf_nodes * leaf_nodes * columns, 6 * leaf_nodes * leaf_nodes),
        pos,
        local_map,
        local_load,
    )
    got = lax.ppermute(send, "c", swap)
    paired = (keep.astype(F32) + got.astype(F32)).astype(BF16)
    pieces, paired = lax.optimization_barrier((pieces, paired))
    maps = call(
        sort_maps,
        jax.ShapeDtypeStruct((3 * n, n // nc), BF16),
        [],
        0,
        (1000, 8 * n * n),
        pieces,
    )
    run_half = lax.all_gather(maps, "y")

    parts = exchange(paired.reshape(nz, width, columns), "z")
    late_map, _ = lax.optimization_barrier((rows_map, maps))
    coupled = call(
        functools.partial(couple_rows, stride=stride),
        jax.ShapeDtypeStruct((width, 2 * n), BF16),
        [pltpu.VMEM((width // 128, interface, 128), F32)],
        0,
        (8 * width * n * n, 4 * width * interface),
        late_map,
        west,
        east,
    )

    loads, faces = call(
        face_parts,
        (
            jax.ShapeDtypeStruct((width, columns), BF16),
            jax.ShapeDtypeStruct((peers, part, 2 * n), BF16),
        ),
        [pltpu.VMEM((2 * n, width), BF16)],
        0,
        (4 * n * width * columns, 4 * n * width),
        parts,
        pieces,
    )
    faces = lax.all_to_all(faces, GRP, 0, 0)
    line = call(
        face_sum,
        jax.ShapeDtypeStruct((ny, part, 2 * n), BF16),
        [],
        0,
        (1000, 4 * n * columns),
        faces,
    )

    all_loads = lax.all_gather(loads, GRP, axis=0, tiled=True)

    run_other = lax.ppermute(run_half, "c", swap)
    line = exchange(line, "y")
    ends, own_maps, own_values = call(
        run_block,
        (
            jax.ShapeDtypeStruct((nx, 3 * n + 2 * part * nc, n // nc), BF16),
            jax.ShapeDtypeStruct((3 * n, n), BF16),
            jax.ShapeDtypeStruct((part, 2 * n), F32),
        ),
        [
            pltpu.VMEM((n, n), F32),
            pltpu.VMEM((n, 2 * n), F32),
            pltpu.VMEM((ny, n, n), F32),
            pltpu.VMEM((part, 2 * n), F32),
            pltpu.VMEM((ny, part, n), F32),
            pltpu.VMEM((3 * n, n), BF16),
        ],
        1,
        (16 * ny * n**3, 6 * ny * n * n),
        at_y,
        line,
        run_half,
        run_other,
    )
    ends = lax.all_to_all(ends, "x", 0, 0)
    other_ends = lax.ppermute(ends, "c", swap)
    met = call(
        meet_values,
        jax.ShapeDtypeStruct((peers, part, 2 * n), BF16),
        [pltpu.VMEM((part, 2 * n), F32)],
        1,
        (12 * nx * n * n * 16, 6 * nx * n * n),
        at_x,
        ends,
        other_ends,
        own_maps,
        own_values,
    )
    met_blocks = lax.all_to_all(met, GRP, 0, 0)

    all_loads, _ = lax.optimization_barrier((all_loads, met))
    initial = jnp.dot(rows_map, all_loads, preferred_element_type=F32)
    met = met_blocks.reshape(columns, 2 * n)
    final = initial + lax.dot_general(coupled, met, NT, preferred_element_type=F32)
    final = jnp.broadcast_to(final.astype(BF16), (nz, width, columns))
    final_own = lax.all_to_all(final, "z", 0, 0).reshape(half, columns)
    final_other = lax.ppermute(final_own, "c", swap)
    result = call(
        leaf_result,
        jax.ShapeDtypeStruct((leaf_nodes, columns), BF16),
        [pltpu.VMEM((interface, columns), F32), pltpu.VMEM((leaf_nodes, columns), F32)],
        1,
        (2 * leaf_nodes * leaf_nodes * columns, 2 * leaf_nodes * leaf_nodes),
        pos,
        final_own,
        final_other,
        local_map,
        local_load,
    )
    return result[None, None]


SPLITS = {(16, 32): (8, 2, 4, 8)}


def solution(mesh):
    shape = SPLITS.get(tuple(mesh.devices.shape), (2, 2, 2, 2))
    split = Mesh(mesh.devices.reshape(shape), ("z", "c", "x", "y"))
    grp, dom = ("z", "c"), ("x", "y")
    return jax.shard_map(
        on_device,
        mesh=split,
        in_specs=(
            P(dom, grp, None, None),
            P(dom, grp, None, None),
            P(dom, grp, None),
            P(dom, grp, None),
            P(dom, None, None),
            P(dom, None, None),
        ),
        out_specs=P(dom, grp, None, None),
        check_vma=False,
    )
```
